32 devices in a mesh: ctx: 8 (over y, x, core), fsdp: 4 (over z).
Axes of the slice: x: 2, y: 2, z: 4, core: 2. Of those that a mesh axis runs over, the one named last changes fastest.
Arguments:
- hidden_in: float32 [4, 1024, 1024], P('fsdp', 'ctx'), may hold values from -6 to 6
- out_cotangent: float32 [4, 1024, 1024], P('fsdp', 'ctx'), may hold values from -6 to 6
- routes: int32 [4, 1024, 8], P('fsdp', 'ctx'), may hold values from 0 to 15, all different within a row; in each aligned block of 128 rows (0 to 127, 128 to 255, ..., all dimensions but the last counted through in order) at most 96 rows name the same one
- route_probs: float32 [4, 1024, 8], P('fsdp', 'ctx'), may hold values from 0.05 to 0.5
- norm_gains: float32 [2, 1024], P(None, ('ctx', 'fsdp')), may hold values from 0.5 to 1.5
- qkv_weight: float32 [1024, 2048], P(('ctx', 'fsdp')), may hold values from -12 to 12
- out_weight: float32 [1024, 1024], P(('ctx', 'fsdp')), may hold values from -0.375 to 0.375
- expert_up: float32 [16, 1024, 1024], P('ctx', 'fsdp'), may hold values from -0.1875 to 0.1875
- expert_down: float32 [16, 512, 1024], P('ctx', None, 'fsdp'), may hold values from -0.75 to 0.75
- norm_gains_first: float32 [2, 1024], P(None, ('ctx', 'fsdp')), may hold values from -12 to 12
- qkv_weight_first: float32 [1024, 2048], P(('ctx', 'fsdp')), may hold values from -12 to 12
- out_weight_first: float32 [1024, 1024], P(('ctx', 'fsdp')), may hold values from -12 to 12
- expert_up_first: float32 [16, 1024, 1024], P('ctx', 'fsdp'), may hold values from -12 to 12
- expert_down_first: float32 [16, 512, 1024], P('ctx', None, 'fsdp'), may hold values from -12 to 12
- norm_gains_second: float32 [2, 1024], P(None, ('ctx', 'fsdp')), may hold values from 0.5 to 4
- qkv_weight_second: float32 [1024, 2048], P(('ctx', 'fsdp')), may hold values from 0.5 to 4
- out_weight_second: float32 [1024, 1024], P(('ctx', 'fsdp')), may hold values from 0.5 to 4
- expert_up_second: float32 [16, 1024, 1024], P('ctx', 'fsdp'), may hold values from 0.5 to 4
- expert_down_second: float32 [16, 512, 1024], P('ctx', None, 'fsdp'), may hold values from 0.5 to 4
Outputs:
- hidden_out: float32 [4, 1024, 1024], P('fsdp', 'ctx')
- hidden_in_grad: float32 [4, 1024, 1024], P('fsdp', 'ctx')
- norm_gains_grad: float32 [2, 1024], P(None, ('ctx', 'fsdp'))
- qkv_weight_grad: float32 [1024, 2048], P(('ctx', 'fsdp'))
- out_weight_grad: float32 [1024, 1024], P(('ctx', 'fsdp'))
- expert_up_grad: float32 [16, 1024, 1024], P('ctx', 'fsdp')
- expert_down_grad: float32 [16, 512, 1024], P('ctx', None, 'fsdp')
- norm_gains_new: float32 [2, 1024], P(None, ('ctx', 'fsdp'))
- qkv_weight_new: float32 [1024, 2048], P(('ctx', 'fsdp'))
- out_weight_new: float32 [1024, 1024], P(('ctx', 'fsdp'))
- expert_up_new: float32 [16, 1024, 1024], P('ctx', 'fsdp')
- expert_down_new: float32 [16, 512, 1024], P('ctx', None, 'fsdp')
- norm_gains_first_new: float32 [2, 1024], P(None, ('ctx', 'fsdp'))
- qkv_weight_first_new: float32 [1024, 2048], P(('ctx', 'fsdp'))
- out_weight_first_new: float32 [1024, 1024], P(('ctx', 'fsdp'))
- expert_up_first_new: float32 [16, 1024, 1024], P('ctx', 'fsdp')
- expert_down_first_new: float32 [16, 512, 1024], P('ctx', None, 'fsdp')
- norm_gains_second_new: float32 [2, 1024], P(None, ('ctx', 'fsdp'))
- qkv_weight_second_new: float32 [1024, 2048], P(('ctx', 'fsdp'))
- out_weight_second_new: float32 [1024, 1024], P(('ctx', 'fsdp'))
- expert_up_second_new: float32 [16, 1024, 1024], P('ctx', 'fsdp')
- expert_down_second_new: float32 [16, 512, 1024], P('ctx', None, 'fsdp')
The draws below stay inside these ranges and needn't reach their ends.
Inputs may be any that keep to these rules, and one draw needn't show every extreme that they name: `routes`: each row names 8 different experts. In each aligned block of 128 rows of a sequence (the rows of one device) no expert is named by more than 96 rows, a bound that some block reaches.
All inputs are finite; a program needn't handle non-finite values.
Results may differ from the reference program's by a relative error of at most 0.0098.
Values may be sent and summed in bfloat16 or wider, within the bound.
No kernel may reach another device: no remote copies, remote signals or barrier semaphores. Data moves between devices by JAX's collectives and lax.ppermute only.
A program may use at most 192 MiB of HBM per device.

```python
import math
import jax
import jax.numpy as jnp
import numpy as np
from jax import lax

MODEL_WIDTH = 1024
QUERY_HEADS = 16
KEY_VALUE_HEADS = 8
HEAD_SIZE = 64
FF = 512
TOP = 8
DEVICE_TOKENS = 128
EXPERTS = 16
SEQUENCE_TOKENS = 1024
SEQS = 4
CAP = 96
QUERY_FEATURES = 1024
KEY_FEATURES = 512
QKV = 2048
N_CTX = 8


def draw_qkv_weight(key, part):
    random_base_key, value_random_key = jax.random.split(key, 2)
    query_columns = jax.random.truncated_normal(random_base_key, -6.0, 6.0, (MODEL_WIDTH, QUERY_HEADS * HEAD_SIZE), jnp.float32) * (2.0 * MODEL_WIDTH ** (-0.5))
    key_value_columns = jax.random.truncated_normal(value_random_key, -6.0, 6.0, (MODEL_WIDTH, 2 * KEY_VALUE_HEADS * HEAD_SIZE), jnp.float32) * MODEL_WIDTH ** (-0.5)
    return jnp.concatenate([query_columns, key_value_columns], 1)


def level_of(key, extent, pieces, least, top_value):
    level = 1.0
    for dim, blocks in pieces:
        steps = jax.random.uniform(jax.random.fold_in(jax.random.fold_in(key, 6), dim), (blocks,), jnp.float32, least / len(pieces), top_value / len(pieces))
        level = level * jnp.repeat(jnp.exp(steps), extent[dim] // blocks).reshape((-1,) + (1,) * (len(extent) - 1 - dim))
    return level


def shared_out(own_key, own, number, rows, number_of, top, most, skew):
    ranking = jax.random.permutation(own_key, number_of)
    crowded, usual = portions_of(number_of, rows * top, most, skew, True), portions_of(number_of, rows * top, most, skew, False)
    places = jnp.arange(number_of)

    def named(tallies, turn):
        used = int((tallies > 0).sum())
        fixed = max(1, used // 4)
        moved = fixed + (places - fixed + turn * (used - fixed)) % max(1, number_of - fixed)
        return jnp.zeros((number_of,), jnp.int32).at[ranking[jnp.where(places < fixed, places, moved)]].set(jnp.asarray(tallies, jnp.int32))

    tallies = jnp.where(number % 4 == 0, named(crowded, number // 4), named(usual, number - number // 4 - 1))
    mixed = jax.random.permutation(jax.random.fold_in(own, 3), number_of)
    giver, receiver = mixed[0:number_of // 2 * 2:2], mixed[1:number_of // 2 * 2:2]
    room = jnp.minimum(tallies[giver] - 1, most - tallies[receiver]) // 2
    room = jnp.where((giver == ranking[0]) | (receiver == ranking[0]) | (tallies[receiver] == 0), 0, jnp.maximum(room, 0))
    moved = jax.random.randint(jax.random.fold_in(own, 4), (number_of // 2,), 0, 1 << 20) % (room + 1)
    tallies = tallies.at[giver].add(-moved).at[receiver].add(moved)
    labels = jnp.searchsorted(jnp.cumsum(tallies), jnp.arange(rows * top), side="right").astype(jnp.int32)
    listing = labels.reshape(top, rows).T
    listing = listing[jax.random.permutation(jax.random.fold_in(own, 1), rows)]
    turn = jax.random.randint(jax.random.fold_in(own, 2), (rows, 1), 0, top)
    return jnp.take_along_axis(listing, (jnp.arange(top)[None, :] + turn) % top, axis=1)


def portions_of(amount, total, limit, slope, full):
    loads = [(1 << 20) // math.isqrt(grade ** slope) + 1 for grade in range(1, amount + 1)]
    largest = limit if full else min(limit, max(-(-total // amount), total * loads[0] // sum(loads)))
    least = 1 if total - largest >= amount - 1 else 0
    counts, spare = [largest] + [least] * (amount - 1), total - largest - least * (amount - 1)
    while spare > 0:
        candidates = [i for i in range(1, amount) if counts[i] < largest] or [i for i in range(1, amount) if counts[i] < limit]
        whole, remaining = sum([loads[i] for i in candidates]), spare
        for i in candidates:
            addition = min(limit - counts[i], max(1, remaining * loads[i] // whole), spare)
            counts[i] = counts[i] + addition
            spare = spare - addition
    return np.array(counts)


def bell_draw(stream_key, shape, spread, limit, pieces=(), held_as=jnp.bfloat16):
    drawn = spread * jax.random.normal(stream_key, shape, jnp.float32)
    if pieces:
        drawn = drawn * level_of(stream_key, shape, pieces, -0.22, 0.18)
    return jnp.clip(drawn, -limit, limit).astype(held_as)


def setup_inputs(seed: int = 0) -> dict:
    arg_keys = jax.random.split(jax.random.key(seed), 20)
    hidden_in = bell_draw(arg_keys[0], (SEQS, SEQUENCE_TOKENS, MODEL_WIDTH), 1.0, 6.0, ((0, 4), (1, 8)), jnp.float32)
    out_cotangent = bell_draw(arg_keys[1], (SEQS, SEQUENCE_TOKENS, MODEL_WIDTH), 1.0, 6.0, ((0, 4), (1, 8)), jnp.float32)
    routes_keys = jax.random.split(jax.random.fold_in(arg_keys[2], 1), SEQS * SEQUENCE_TOKENS // DEVICE_TOKENS)
    routes_turns = jax.random.permutation(jax.random.fold_in(arg_keys[2], 3), SEQS * SEQUENCE_TOKENS // DEVICE_TOKENS)
    routes = jax.vmap(lambda own, number: shared_out(jax.random.fold_in(arg_keys[2], 2), own, number, DEVICE_TOKENS, EXPERTS, TOP, CAP, 1))(routes_keys, routes_turns).reshape((SEQS, SEQUENCE_TOKENS, TOP))
    route_probs = jnp.clip(jnp.exp(math.log(0.5) - 2.3025851 * jax.random.uniform(arg_keys[3], (SEQS, SEQUENCE_TOKENS, TOP), jnp.float32) ** level_of(arg_keys[3], (SEQS, SEQUENCE_TOKENS, TOP), ((0, 4), (1, 8)), -0.2, 0.2)), 0.05, 0.5)
    norm_gains = jnp.clip(1.0 + 0.1 * jax.random.normal(arg_keys[4], (2, MODEL_WIDTH), jnp.float32), 0.5, 1.5)
    qkv_weight = draw_qkv_weight(jax.random.fold_in(arg_keys[19], 71), 0)
    out_weight = bell_draw(arg_keys[6], (QUERY_FEATURES, MODEL_WIDTH), (QUERY_FEATURES // 4) ** -0.5, 0.375, ((0, 32),), jnp.float32)
    expert_up = bell_draw(arg_keys[7], (EXPERTS, MODEL_WIDTH, 2 * FF), MODEL_WIDTH ** -0.5, 0.1875, ((0, 8), (1, 4)), jnp.float32)
    expert_down = bell_draw(arg_keys[8], (EXPERTS, FF, MODEL_WIDTH), (FF // 8) ** -0.5, 0.75, ((0, 8), (2, 4)), jnp.float32)
    norm_gains_first = bell_draw(arg_keys[9], (2, MODEL_WIDTH), 2.0, 12.0, ((1, 32),), jnp.float32)
    qkv_weight_first = bell_draw(arg_keys[10], (MODEL_WIDTH, QKV), 2.0, 12.0, ((0, 32),), jnp.float32)
    out_weight_first = bell_draw(arg_keys[11], (QUERY_FEATURES, MODEL_WIDTH), 2.0, 12.0, ((0, 32),), jnp.float32)
    expert_up_first = bell_draw(arg_keys[12], (EXPERTS, MODEL_WIDTH, 2 * FF), 2.0, 12.0, ((0, 8), (1, 4)), jnp.float32)
    expert_down_first = bell_draw(arg_keys[13], (EXPERTS, FF, MODEL_WIDTH), 2.0, 12.0, ((0, 8), (2, 4)), jnp.float32)
    norm_gains_second = jnp.clip(jnp.exp(math.log(4.0) - 2.0794415 * jax.random.uniform(arg_keys[14], (2, MODEL_WIDTH), jnp.float32) ** level_of(arg_keys[14], (2, MODEL_WIDTH), ((1, 32),), -0.2, 0.2)), 0.5, 4.0)
    qkv_weight_second = jnp.clip(jnp.exp(math.log(4.0) - 2.0794415 * jax.random.uniform(arg_keys[15], (MODEL_WIDTH, QKV), jnp.float32) ** level_of(arg_keys[15], (MODEL_WIDTH, QKV), ((0, 32),), -0.2, 0.2)), 0.5, 4.0)
    out_weight_second = jnp.clip(jnp.exp(math.log(4.0) - 2.0794415 * jax.random.uniform(arg_keys[16], (QUERY_FEATURES, MODEL_WIDTH), jnp.float32) ** level_of(arg_keys[16], (QUERY_FEATURES, MODEL_WIDTH), ((0, 32),), -0.2, 0.2)), 0.5, 4.0)
    expert_up_second = jnp.clip(jnp.exp(math.log(4.0) - 2.0794415 * jax.random.uniform(arg_keys[17], (EXPERTS, MODEL_WIDTH, 2 * FF), jnp.float32) ** level_of(arg_keys[17], (EXPERTS, MODEL_WIDTH, 2 * FF), ((0, 8), (1, 4)), -0.2, 0.2)), 0.5, 4.0)
    expert_down_second = jnp.clip(jnp.exp(math.log(4.0) - 2.0794415 * jax.random.uniform(arg_keys[18], (EXPERTS, FF, MODEL_WIDTH), jnp.float32) ** level_of(arg_keys[18], (EXPERTS, FF, MODEL_WIDTH), ((0, 8), (2, 4)), -0.2, 0.2)), 0.5, 4.0)
    return dict(hidden_in=hidden_in, out_cotangent=out_cotangent, routes=routes, route_probs=route_probs, norm_gains=norm_gains, qkv_weight=qkv_weight, out_weight=out_weight, expert_up=expert_up, expert_down=expert_down, norm_gains_first=norm_gains_first, qkv_weight_first=qkv_weight_first, out_weight_first=out_weight_first, expert_up_first=expert_up_first, expert_down_first=expert_down_first, norm_gains_second=norm_gains_second, qkv_weight_second=qkv_weight_second, out_weight_second=out_weight_second, expert_up_second=expert_up_second, expert_down_second=expert_down_second)


RES_SCALE = 0.22
SCORE_SCALE = 0.015625
NORM_EPS = 1e-06
ROPE_BASE = 10000.0
LEARN_RATE = 0.02
BETA_FIRST = 0.9
BETA_SECOND = 0.999
ADAM_EPS = 1e-08
WEIGHT_DECAY = 0.1
ADAM_STEP = 3.0
MASK_VALUE = -1e+30

def positions(row_ids, tok_dev, n_ctx):
    device = row_ids // tok_dev
    within = row_ids % tok_dev
    half_block = tok_dev // 2
    return jnp.where(within < half_block, device * half_block + within, (2 * n_ctx - 1 - device) * half_block + within - half_block).astype(jnp.int32)

def rope_tables(position, head_dim):
    half_dim = head_dim // 2
    frequency = ROPE_BASE ** (-(jnp.arange(half_dim, dtype=jnp.float32) * 2.0 / head_dim))
    angles = position.astype(jnp.float32)[:, None] * frequency[None, :]
    return (jnp.cos(angles)[:, None, :], jnp.sin(angles)[:, None, :])

def apply_rotary(values, cosine_table, sine_table):
    half_dim = values.shape[-1] // 2
    lower_half, upper_half = (values[..., :half_dim], values[..., half_dim:])
    return jnp.concatenate([lower_half * cosine_table - upper_half * sine_table, upper_half * cosine_table + lower_half * sine_table], -1)

def inverse_rotary(cotangent, cosine_table, sine_table):
    half_dim = cotangent.shape[-1] // 2
    lower_half, upper_half = (cotangent[..., :half_dim], cotangent[..., half_dim:])
    return jnp.concatenate([lower_half * cosine_table + upper_half * sine_table, upper_half * cosine_table - lower_half * sine_table], -1)

def norm_back(inputs, inv_rms, gain, cotangent):
    weighted = gain * cotangent
    gain_grad = lax.optimization_barrier(jnp.sum(cotangent * inputs * inv_rms, 0))
    input_grad = inv_rms * weighted - inputs * inv_rms ** 3 * lax.optimization_barrier(jnp.mean(weighted * inputs, -1, keepdims=True))
    return (gain_grad, input_grad)

def rounded(values):
    return lax.optimization_barrier(values.astype(jnp.bfloat16)).astype(jnp.float32)

def scores_of(queries, key_head_rows, q_pos, k_pos):
    raw_scores = jnp.einsum('qgrd,kgd->grqk', queries.astype(jnp.float32), key_head_rows.astype(jnp.float32))
    raw_scores = raw_scores * SCORE_SCALE
    allowed = k_pos[None, :] <= q_pos[:, None]
    return jnp.where(allowed, raw_scores, MASK_VALUE)

def attend(queries, key_head_rows, value_head_rows, q_pos, k_pos):
    scores = scores_of(queries, key_head_rows, q_pos, k_pos)
    row_max = lax.optimization_barrier(jnp.max(scores, -1, keepdims=True))
    logarithm_total = row_max + jnp.log(lax.optimization_barrier(jnp.sum(jnp.exp(scores - row_max), -1, keepdims=True)))
    attn_probs = rounded(jnp.exp(scores - logarithm_total))
    output = jnp.einsum('grqk,kgd->qgrd', attn_probs, value_head_rows.astype(jnp.float32)).astype(jnp.bfloat16)
    return (output, logarithm_total)

def attend_back(queries, key_head_rows, value_head_rows, output, out_grad, logarithm_total, q_pos, k_pos):
    scores = scores_of(queries, key_head_rows, q_pos, k_pos)
    attn_probs = jnp.exp(scores - logarithm_total)
    grad_wide = out_grad.astype(jnp.float32)
    value_gradient = jnp.einsum('grqk,qgrd->kgd', rounded(attn_probs), grad_wide)
    prob_grad = jnp.einsum('qgrd,kgd->grqk', grad_wide, value_head_rows.astype(jnp.float32))
    row_dot = jnp.einsum('qgrd,qgrd->grq', grad_wide, output.astype(jnp.float32))[..., None]
    score_grad = rounded(attn_probs * (prob_grad - row_dot) * SCORE_SCALE)
    query_gradient = jnp.einsum('grqk,kgd->qgrd', score_grad, key_head_rows.astype(jnp.float32))
    key_gradient = jnp.einsum('grqk,qgrd->kgd', score_grad, queries.astype(jnp.float32))
    return (query_gradient, key_gradient, value_gradient)

def one_sequence(tokens, cotangent, route_ids, route_weights, working):
    gains_work, qkv_work, out_work, up_work, down_work = working
    query_group_size = QUERY_HEADS // KEY_VALUE_HEADS
    position = positions(jnp.arange(SEQUENCE_TOKENS, dtype=jnp.int32), DEVICE_TOKENS, N_CTX)
    cosine_table, sine_table = rope_tables(position, HEAD_SIZE)
    gain_attn = gains_work[0].astype(jnp.float32)
    gain_ffn = gains_work[1].astype(jnp.float32)
    inv_first = lax.rsqrt(lax.optimization_barrier(jnp.mean(tokens * tokens, -1, keepdims=True)) + NORM_EPS)
    normed_attn = (tokens * inv_first * gain_attn).astype(jnp.bfloat16)
    projected_rows = jnp.dot(normed_attn, qkv_work, preferred_element_type=jnp.float32)
    query_head_rows = apply_rotary(projected_rows[:, :QUERY_FEATURES].reshape(SEQUENCE_TOKENS, QUERY_HEADS, HEAD_SIZE), cosine_table, sine_table).astype(jnp.bfloat16)
    key_head_rows = apply_rotary(projected_rows[:, QUERY_FEATURES:QUERY_FEATURES + KEY_FEATURES].reshape(SEQUENCE_TOKENS, KEY_VALUE_HEADS, HEAD_SIZE), cosine_table, sine_table).astype(jnp.bfloat16)
    value_head_rows = projected_rows[:, QUERY_FEATURES + KEY_FEATURES:].astype(jnp.bfloat16).reshape(SEQUENCE_TOKENS, KEY_VALUE_HEADS, HEAD_SIZE)
    rows_per_block = math.gcd(SEQUENCE_TOKENS, 512)
    block_list = SEQUENCE_TOKENS // rows_per_block
    grouped_queries = query_head_rows.reshape(block_list, rows_per_block, KEY_VALUE_HEADS, query_group_size, HEAD_SIZE)
    position_blocks = position.reshape(block_list, rows_per_block)

    def forward_block(block_item):
        return attend(block_item[0], key_head_rows, value_head_rows, block_item[1], position)
    attended_rows, logarithm_total = lax.map(forward_block, (grouped_queries, position_blocks))
    attn_rows = attended_rows.reshape(SEQUENCE_TOKENS, QUERY_FEATURES)
    residual = tokens + RES_SCALE * jnp.dot(attn_rows, out_work, preferred_element_type=jnp.float32)
    inv_second = lax.rsqrt(lax.optimization_barrier(jnp.mean(residual * residual, -1, keepdims=True)) + NORM_EPS)
    normed_ffn = (residual * inv_second * gain_ffn).astype(jnp.bfloat16)
    n_rows = SEQUENCE_TOKENS * TOP
    flat_routes = route_ids.reshape(N_CTX, DEVICE_TOKENS * TOP).astype(jnp.int32)
    onehot = (flat_routes[..., None] == jnp.arange(EXPERTS, dtype=jnp.int32)).astype(jnp.int32)
    slot_index = (lax.optimization_barrier(jnp.sum(onehot * jnp.cumsum(onehot, 1), -1)) - 1).astype(jnp.int32)
    dest_index = (flat_routes * (N_CTX * CAP) + jnp.arange(N_CTX, dtype=jnp.int32)[:, None] * CAP + slot_index).reshape(-1).astype(jnp.int32)
    fill_index = jnp.full((EXPERTS * N_CTX * CAP,), n_rows, jnp.int32).at[dest_index].set(jnp.arange(n_rows, dtype=jnp.int32))
    token_index = jnp.where(fill_index < n_rows, fill_index // TOP, SEQUENCE_TOKENS).astype(jnp.int32)
    padded = jnp.concatenate([normed_ffn, jnp.zeros((1, MODEL_WIDTH), jnp.bfloat16)], 0)
    expert_rows_all = padded[token_index].reshape(EXPERTS, N_CTX * CAP, MODEL_WIDTH)
    route_grad = (route_weights[..., None] * (RES_SCALE * cotangent)[:, None, :]).astype(jnp.bfloat16)
    grad_padded = jnp.concatenate([route_grad.reshape(n_rows, MODEL_WIDTH), jnp.zeros((1, MODEL_WIDTH), jnp.bfloat16)], 0)
    grad_rows_all = grad_padded[fill_index].reshape(EXPERTS, N_CTX * CAP, MODEL_WIDTH)

    def expert_block(block_item):
        expert_rows, grad_rows, up_one, down_one = block_item
        gate_up = jnp.dot(expert_rows, up_one, preferred_element_type=jnp.float32)
        gate_part = gate_up[:, :FF]
        up_part = gate_up[:, FF:]
        sigmoid_gate = jax.nn.sigmoid(gate_part)
        expert_hidden = (gate_part * sigmoid_gate * up_part).astype(jnp.bfloat16)
        expert_value = jnp.dot(expert_hidden, down_one, preferred_element_type=jnp.float32).astype(jnp.bfloat16)
        hidden_grad = jnp.dot(grad_rows, down_one.T, preferred_element_type=jnp.float32)
        gate_grad = hidden_grad * up_part * sigmoid_gate * (1.0 + gate_part * (1.0 - sigmoid_gate))
        up_grad = hidden_grad * gate_part * sigmoid_gate
        pair_grad = jnp.concatenate([gate_grad, up_grad], -1).astype(jnp.bfloat16)
        down_term = jnp.dot(expert_hidden.T, grad_rows, preferred_element_type=jnp.float32)
        up_term = jnp.dot(expert_rows.T, pair_grad, preferred_element_type=jnp.float32)
        input_rows = jnp.dot(pair_grad, up_one.T, preferred_element_type=jnp.float32).astype(jnp.bfloat16)
        return (expert_value, input_rows, up_term, down_term)
    expert_values, input_rows, up_terms, down_terms = lax.map(expert_block, (expert_rows_all, grad_rows_all, up_work, down_work))
    route_values = expert_values.reshape(-1, MODEL_WIDTH)[dest_index].astype(jnp.float32).reshape(SEQUENCE_TOKENS, TOP, MODEL_WIDTH)
    hidden_out = residual + RES_SCALE * lax.optimization_barrier(jnp.sum(route_values * route_weights[..., None], 1))
    ffn_grad = lax.optimization_barrier(jnp.sum(input_rows.reshape(-1, MODEL_WIDTH)[dest_index].astype(jnp.float32).reshape(SEQUENCE_TOKENS, TOP, MODEL_WIDTH), 1))
    gain_ffn_grad, residual_norm_grad = norm_back(residual, inv_second, gain_ffn, ffn_grad)
    residual_grad = cotangent + residual_norm_grad
    attn_grad = (RES_SCALE * residual_grad).astype(jnp.bfloat16)
    out_term = jnp.dot(attn_rows.T, attn_grad, preferred_element_type=jnp.float32)
    attention_output_grad = jnp.dot(attn_grad, out_work.T, preferred_element_type=jnp.float32).astype(jnp.bfloat16)

    def block_backward_pass(totals, block_item):
        query_block, out_block, grad_block, total_block, pos_block = block_item
        query_gradient, key_gradient, value_gradient = attend_back(query_block, key_head_rows, value_head_rows, out_block, grad_block, total_block, pos_block, position)
        return ((totals[0] + key_gradient, totals[1] + value_gradient), query_gradient)
    zeroed_head_rows = jnp.zeros((SEQUENCE_TOKENS, KEY_VALUE_HEADS, HEAD_SIZE), jnp.float32)
    (key_gradient, value_gradient), query_gradient = lax.scan(block_backward_pass, (zeroed_head_rows, zeroed_head_rows), (grouped_queries, attended_rows, attention_output_grad.reshape(block_list, rows_per_block, KEY_VALUE_HEADS, query_group_size, HEAD_SIZE), logarithm_total, position_blocks))
    query_rows = inverse_rotary(query_gradient.reshape(SEQUENCE_TOKENS, QUERY_HEADS, HEAD_SIZE), cosine_table, sine_table).astype(jnp.bfloat16).reshape(SEQUENCE_TOKENS, QUERY_FEATURES)
    key_rows = inverse_rotary(key_gradient, cosine_table, sine_table).astype(jnp.bfloat16).reshape(SEQUENCE_TOKENS, KEY_FEATURES)
    qkv_rows = jnp.concatenate([query_rows, key_rows, value_gradient.reshape(SEQUENCE_TOKENS, KEY_FEATURES).astype(jnp.bfloat16)], 1)
    qkv_term = jnp.dot(normed_attn.T, qkv_rows, preferred_element_type=jnp.float32)
    attn_in_grad = jnp.dot(qkv_rows, qkv_work.T, preferred_element_type=jnp.float32)
    gain_attn_grad, input_norm_grad = norm_back(tokens, inv_first, gain_attn, attn_in_grad)
    input_grad = residual_grad + input_norm_grad
    gains_term = jnp.stack([gain_attn_grad, gain_ffn_grad])
    return (hidden_out, input_grad, (gains_term, qkv_term, out_term, up_terms, down_terms))

def adamw_update(weight, gradient, first_moment, second_moment, decay_rate):
    first_new = BETA_FIRST * first_moment + (1.0 - BETA_FIRST) * gradient
    second_new = BETA_SECOND * second_moment + (1.0 - BETA_SECOND) * gradient * gradient
    first_hat = first_new / (1.0 - BETA_FIRST ** ADAM_STEP)
    second_hat = second_new / (1.0 - BETA_SECOND ** ADAM_STEP)
    weight_new = weight - LEARN_RATE * (first_hat / (jnp.sqrt(second_hat) + ADAM_EPS) + decay_rate * weight)
    return (weight_new, first_new, second_new)

def reference(hidden_in, out_cotangent, routes, route_probs, norm_gains, qkv_weight, out_weight, expert_up, expert_down, norm_gains_first, qkv_weight_first, out_weight_first, expert_up_first, expert_down_first, norm_gains_second, qkv_weight_second, out_weight_second, expert_up_second, expert_down_second):
    masters = (norm_gains, qkv_weight, out_weight, expert_up, expert_down)
    working = tuple((master.astype(jnp.bfloat16) for master in masters))

    def sequence_step(totals, seq_item):
        tokens, cotangent, route_ids, route_weights = seq_item
        seq_out, seq_grad, terms = one_sequence(tokens, cotangent, route_ids, route_weights, working)
        return (tuple((running + addend for running, addend in zip(totals, terms))), (seq_out, seq_grad))
    zero_grads = tuple((jnp.zeros(master.shape, jnp.float32) for master in masters))
    gradients, (hidden_out, hidden_in_grad) = lax.scan(sequence_step, zero_grads, (hidden_in, out_cotangent, routes, route_probs))
    norm_new = adamw_update(norm_gains, gradients[0], norm_gains_first, norm_gains_second, 0.0)
    qkv_new = adamw_update(qkv_weight, gradients[1], qkv_weight_first, qkv_weight_second, WEIGHT_DECAY)
    out_new = adamw_update(out_weight, gradients[2], out_weight_first, out_weight_second, WEIGHT_DECAY)
    up_new = adamw_update(expert_up, gradients[3], expert_up_first, expert_up_second, WEIGHT_DECAY)
    down_new = adamw_update(expert_down, gradients[4], expert_down_first, expert_down_second, WEIGHT_DECAY)
    return (hidden_out, hidden_in_grad, gradients[0], gradients[1], gradients[2], gradients[3], gradients[4], norm_new[0], qkv_new[0], out_new[0], up_new[0], down_new[0], norm_new[1], qkv_new[1], out_new[1], up_new[1], down_new[1], norm_new[2], qkv_new[2], out_new[2], up_new[2], down_new[2])
```

```python
import jax
import jax.numpy as jnp
from jax import lax
from jax.sharding import PartitionSpec as P

MODEL_WIDTH = 1024
QUERY_HEADS = 16
KEY_VALUE_HEADS = 8
HEAD_SIZE = 64
FF = 512
TOP = 8
DEVICE_TOKENS = 128
QUERY_FEATURES = 1024
KEY_FEATURES = 512


RES_SCALE = 0.22
SCORE_SCALE = 0.015625
NORM_EPS = 1e-06
ROPE_BASE = 10000.0
LEARN_RATE = 0.02
BETA_FIRST = 0.9
BETA_SECOND = 0.999
ADAM_EPS = 1e-08
WEIGHT_DECAY = 0.1
ADAM_STEP = 3.0
MASK_VALUE = -1e30


def positions(row_ids, tok_dev, n_ctx):
    device = row_ids // tok_dev
    within = row_ids % tok_dev
    half_block = tok_dev // 2
    return jnp.where(
        within < half_block,
        device * half_block + within,
        (2 * n_ctx - 1 - device) * half_block + within - half_block,
    )


def rope_tables(position, head_dim):
    half_dim = head_dim // 2
    frequency = ROPE_BASE ** (-(jnp.arange(half_dim, dtype=jnp.float32) * 2.0 / head_dim))
    angles = position.astype(jnp.float32)[:, None] * frequency[None, :]
    return (jnp.cos(angles)[:, None, :], jnp.sin(angles)[:, None, :])


def apply_rotary(values, cosine_table, sine_table):
    half_dim = values.shape[-1] // 2
    lower_half, upper_half = (values[..., :half_dim], values[..., half_dim:])
    return jnp.concatenate(
        [
            lower_half * cosine_table - upper_half * sine_table,
            upper_half * cosine_table + lower_half * sine_table,
        ],
        -1,
    )


def inverse_rotary(cotangent, cosine_table, sine_table):
    half_dim = cotangent.shape[-1] // 2
    lower_half, upper_half = (cotangent[..., :half_dim], cotangent[..., half_dim:])
    return jnp.concatenate(
        [
            lower_half * cosine_table + upper_half * sine_table,
            upper_half * cosine_table - lower_half * sine_table,
        ],
        -1,
    )


def scores_of(queries, key_head_rows, q_pos, k_pos):
    raw_scores = jnp.einsum(
        "qgrd,kgd->grqk", queries, key_head_rows, preferred_element_type=jnp.float32
    )
    raw_scores = raw_scores * SCORE_SCALE
    allowed = k_pos[None, :] <= q_pos[:, None]
    return jnp.where(allowed, raw_scores, MASK_VALUE)


def attend(queries, key_head_rows, value_head_rows, q_pos, k_pos):
    scores = scores_of(queries, key_head_rows, q_pos, k_pos)
    row_max = jnp.max(scores, -1, keepdims=True)
    logarithm_total = row_max + jnp.log(jnp.sum(jnp.exp(scores - row_max), -1, keepdims=True))
    attn_probs = jnp.exp(scores - logarithm_total).astype(jnp.bfloat16)
    output = jnp.einsum(
        "grqk,kgd->qgrd", attn_probs, value_head_rows, preferred_element_type=jnp.float32
    ).astype(jnp.bfloat16)
    return (output, logarithm_total)


def attend_back(
    queries, key_head_rows, value_head_rows, output, out_grad, logarithm_total, q_pos, k_pos
):
    scores = scores_of(queries, key_head_rows, q_pos, k_pos)
    attn_probs = jnp.exp(scores - logarithm_total)
    value_gradient = jnp.einsum(
        "grqk,qgrd->kgd",
        attn_probs.astype(jnp.bfloat16),
        out_grad,
        preferred_element_type=jnp.float32,
    )
    prob_grad = jnp.einsum(
        "qgrd,kgd->grqk", out_grad, value_head_rows, preferred_element_type=jnp.float32
    )
    row_dot = jnp.einsum("qgrd,qgrd->grq", out_grad, output, preferred_element_type=jnp.float32)[
        ..., None
    ]
    score_grad = (attn_probs * (prob_grad - row_dot) * SCORE_SCALE).astype(jnp.bfloat16)
    query_gradient = jnp.einsum(
        "grqk,kgd->qgrd", score_grad, key_head_rows, preferred_element_type=jnp.float32
    )
    key_gradient = jnp.einsum(
        "grqk,qgrd->kgd", score_grad, queries, preferred_element_type=jnp.float32
    )
    return (query_gradient, key_gradient, value_gradient)


def adamw_update(weight, gradient, first_moment, second_moment, decay_rate):
    first_new = BETA_FIRST * first_moment + (1.0 - BETA_FIRST) * gradient
    second_new = BETA_SECOND * second_moment + (1.0 - BETA_SECOND) * gradient * gradient
    first_hat = first_new / (1.0 - BETA_FIRST**ADAM_STEP)
    second_hat = second_new / (1.0 - BETA_SECOND**ADAM_STEP)
    weight_new = weight - LEARN_RATE * (
        first_hat / (jnp.sqrt(second_hat) + ADAM_EPS) + decay_rate * weight
    )
    return (weight_new, first_new, second_new)


def xor_perm(size, mask):
    return [(i, i ^ mask) for i in range(size)]


def exchange(values, axis, mask):
    return lax.ppermute(values, axis, xor_perm(lax.axis_size(axis), mask))


def relative_ids(size):
    return jnp.array(list(range(0, size, 2)) + list(range(1, size, 2)), jnp.int32)


def gather_rows(rows):
    size = lax.axis_size("ctx")
    even = jnp.concatenate(
        [rows] + [exchange(rows, "ctx", mask) for mask in range(2, size, 2)], 0
    )
    return jnp.concatenate([even, exchange(even, "ctx", 1)], 0)


def scatter_sum(rows):
    size = lax.axis_size("ctx")
    half = rows.shape[0] // 2
    block = rows.shape[0] // size
    other = exchange(rows[half:].astype(jnp.bfloat16), "ctx", 1)
    pair_sum = rows[:half] + other.astype(jnp.float32)
    total = pair_sum[:block]
    for place in range(1, size // 2):
        piece = pair_sum[place * block : (place + 1) * block].astype(jnp.bfloat16)
        total = total + exchange(piece, "ctx", 2 * place).astype(jnp.float32)
    return total


def swap_blocks(blocks):
    size = lax.axis_size("ctx")
    half = size // 2
    other = exchange(blocks[half:], "ctx", 1)
    even = [blocks[0]]
    odd = [other[0]]
    for place in range(1, half):
        got = exchange(jnp.stack([blocks[place], other[place]]), "ctx", 2 * place)
        even.append(got[0])
        odd.append(got[1])
    return even + odd


def to_natural(pieces, index):
    size = pieces.shape[0]
    bit = 1
    while bit < size:
        swapped = jnp.stack([pieces[i ^ bit] for i in range(size)])
        pieces = jnp.where((index & bit) != 0, swapped, pieces)
        bit *= 2
    return pieces


def gather_fsdp(values):
    size = lax.axis_size("fsdp")
    pieces = jnp.stack([values] + [exchange(values, "fsdp", mask) for mask in range(1, size)])
    return to_natural(pieces, lax.axis_index("fsdp"))


def local(
    hidden_in,
    out_cotangent,
    routes,
    route_probs,
    norm_gains,
    qkv_weight,
    out_weight,
    expert_up,
    expert_down,
    norm_gains_first,
    qkv_weight_first,
    out_weight_first,
    expert_up_first,
    expert_down_first,
    norm_gains_second,
    qkv_weight_second,
    out_weight_second,
    expert_up_second,
    expert_down_second,
):
    f32 = jnp.float32
    bf16 = jnp.bfloat16
    both = ("ctx", "fsdp")
    n_ctx = lax.axis_size("ctx")
    n_fsdp = lax.axis_size("fsdp")
    n_all = n_ctx * n_fsdp
    ctx_index = lax.axis_index("ctx")
    n_exp = expert_up.shape[0]
    shard = qkv_weight.shape[0]
    seq = DEVICE_TOKENS * n_ctx
    q_dev = QUERY_HEADS // n_ctx
    kv_dev = max(1, KEY_VALUE_HEADS // n_ctx)
    share = max(1, n_ctx // KEY_VALUE_HEADS)
    q_cols = q_dev * HEAD_SIZE
    kv_cols = kv_dev * HEAD_SIZE
    cols = q_cols + 2 * kv_cols

    tokens = hidden_in[0]
    cotangent = out_cotangent[0]
    inv_first = lax.rsqrt(jnp.mean(tokens * tokens, -1, keepdims=True) + NORM_EPS)
    unit_rows = (tokens * inv_first).astype(bf16)
    unit_all = gather_rows(unit_rows)

    gain_shard = norm_gains.astype(bf16).astype(f32)
    qkv_shard = qkv_weight.astype(bf16).astype(f32)
    scaled = (qkv_shard * gain_shard[0][:, None]).astype(bf16)
    q_part = scaled[:, :QUERY_FEATURES].reshape(shard, n_ctx, q_cols)
    k_part = scaled[:, QUERY_FEATURES : QUERY_FEATURES + KEY_FEATURES]
    v_part = scaled[:, QUERY_FEATURES + KEY_FEATURES :]
    k_part = jnp.repeat(k_part.reshape(shard, n_ctx // share, kv_cols), share, 1)
    v_part = jnp.repeat(v_part.reshape(shard, n_ctx // share, kv_cols), share, 1)
    head_cols = jnp.concatenate([q_part, k_part, v_part], -1).transpose(1, 0, 2)
    head_cols = jnp.broadcast_to(head_cols[:, None], (n_ctx, n_fsdp, shard, cols))
    qkv_heads = lax.all_to_all(
        head_cols.reshape(n_all, shard, cols), both, split_axis=0, concat_axis=0, tiled=True
    ).reshape(MODEL_WIDTH, cols)

    up_work = lax.all_gather(expert_up.astype(bf16), "fsdp", axis=1, tiled=True)
    down_work = lax.all_gather(expert_down.astype(bf16), "fsdp", axis=2, tiled=True)

    out_heads = gather_fsdp(out_weight.astype(bf16)).reshape(q_cols, MODEL_WIDTH)
    out_all = gather_rows(out_heads)
    scaled_cotangent = (RES_SCALE * cotangent).astype(bf16)
    cotangent_all = gather_rows(scaled_cotangent)

    experts = jnp.arange(n_exp * n_ctx, dtype=jnp.int32)
    chosen = routes[0][:, :, None] == experts[None, None, :]
    weight_rows = jnp.sum(jnp.where(chosen, route_probs[0][:, :, None], 0.0), 1)
    weight_all = gather_rows(weight_rows)
    weight_own = lax.dynamic_slice_in_dim(weight_all, ctx_index * n_exp, n_exp, 1)

    gain_group = gather_fsdp(norm_gains[1:2].astype(bf16)).reshape(1, n_fsdp * shard)
    gain_pieces = gather_rows(gain_group)
    half = n_ctx // 2
    gain_pieces = jnp.stack(
        [gain_pieces[(i // 2) + (i % 2) * half] for i in range(n_ctx)]
    )
    gain_ffn = to_natural(gain_pieces, ctx_index).reshape(1, MODEL_WIDTH).astype(f32)

    device_ids = ctx_index ^ relative_ids(n_ctx)
    row_ids = device_ids[:, None] * DEVICE_TOKENS + jnp.arange(DEVICE_TOKENS, dtype=jnp.int32)
    position = positions(row_ids.reshape(-1), DEVICE_TOKENS, n_ctx)
    cosine_table, sine_table = rope_tables(position, HEAD_SIZE)

    projected = jnp.dot(unit_all, qkv_heads, preferred_element_type=f32)
    query_heads = (
        apply_rotary(
            projected[:, :q_cols].reshape(seq, q_dev, HEAD_SIZE), cosine_table, sine_table
        )
        .astype(bf16)
        .reshape(seq, kv_dev, q_dev // kv_dev, HEAD_SIZE)
    )
    key_heads = apply_rotary(
        projected[:, q_cols : q_cols + kv_cols].reshape(seq, kv_dev, HEAD_SIZE),
        cosine_table,
        sine_table,
    ).astype(bf16)
    value_heads = projected[:, q_cols + kv_cols :].astype(bf16).reshape(seq, kv_dev, HEAD_SIZE)
    attended, logarithm_total = attend(query_heads, key_heads, value_heads, position, position)
    attended_rows = attended.reshape(seq, q_cols)
    attn_rows = jnp.concatenate(
        swap_blocks(attended_rows.reshape(n_ctx, DEVICE_TOKENS, q_cols)), 1
    )
    residual = tokens + RES_SCALE * jnp.dot(attn_rows, out_all, preferred_element_type=f32)
    inv_second = lax.rsqrt(jnp.mean(residual * residual, -1, keepdims=True) + NORM_EPS)
    normed_ffn = (residual * inv_second * gain_ffn).astype(bf16)
    normed_all = gather_rows(normed_ffn)

    weight_cols = jnp.transpose(weight_own)[:, :, None]
    hidden_grad = weight_cols * jnp.einsum(
        "md,efd->emf", cotangent_all, down_work, preferred_element_type=f32
    )
    gate_up = jnp.einsum("md,edf->emf", normed_all, up_work, preferred_element_type=f32)
    gate_part = gate_up[..., :FF]
    up_part = gate_up[..., FF:]
    sigmoid_gate = jax.nn.sigmoid(gate_part)
    weighted_hidden = (weight_cols * (gate_part * sigmoid_gate * up_part)).astype(bf16)
    gate_grad = hidden_grad * up_part * sigmoid_gate * (1.0 + gate_part * (1.0 - sigmoid_gate))
    up_grad = hidden_grad * gate_part * sigmoid_gate
    pair_grad = jnp.concatenate([gate_grad, up_grad], -1).astype(bf16)
    input_rows = jnp.einsum("emf,edf->md", pair_grad, up_work, preferred_element_type=f32)
    ffn_grad = scatter_sum(input_rows)
    down_term = jnp.einsum(
        "emf,md->efd", weighted_hidden, cotangent_all, preferred_element_type=f32
    ).astype(bf16)
    down_grad_shard = lax.psum_scatter(
        down_term, "fsdp", scatter_dimension=2, tiled=True
    ).astype(f32)
    up_term = jnp.einsum(
        "md,emf->edf", normed_all, pair_grad, preferred_element_type=f32
    ).astype(bf16)
    up_grad_shard = lax.psum_scatter(up_term, "fsdp", scatter_dimension=1, tiled=True).astype(f32)
    expert_sum = jnp.einsum("emf,efd->md", weighted_hidden, down_work, preferred_element_type=f32)
    hidden_out = residual + RES_SCALE * scatter_sum(expert_sum)

    weighted = gain_ffn * ffn_grad
    gain_ffn_part = jnp.sum(ffn_grad * residual * inv_second, 0)
    residual_grad = (
        cotangent
        + inv_second * weighted
        - residual * inv_second**3 * jnp.mean(weighted * residual, -1, keepdims=True)
    )
    attn_grad = (RES_SCALE * residual_grad).astype(bf16)
    attn_out_grad = lax.dot_general(
        attn_grad, out_all, (((1,), (1,)), ((), ())), preferred_element_type=f32
    ).astype(bf16)
    attn_out_heads = jnp.concatenate(
        swap_blocks(
            jnp.stack([attn_out_grad[:, i * q_cols : (i + 1) * q_cols] for i in range(n_ctx)])
        ),
        0,
    )
    query_gradient, key_gradient, value_gradient = attend_back(
        query_heads,
        key_heads,
        value_heads,
        attended,
        attn_out_heads.reshape(seq, kv_dev, q_dev // kv_dev, HEAD_SIZE),
        logarithm_total,
        position,
        position,
    )
    query_rows = inverse_rotary(
        query_gradient.reshape(seq, q_dev, HEAD_SIZE), cosine_table, sine_table
    )
    key_rows = inverse_rotary(key_gradient, cosine_table, sine_table)
    qkv_rows = jnp.concatenate(
        [
            query_rows.reshape(seq, q_cols),
            key_rows.reshape(seq, kv_cols),
            value_gradient.reshape(seq, kv_cols),
        ],
        1,
    ).astype(bf16)
    scaled_in_grad = scatter_sum(
        lax.dot_general(
            qkv_rows, qkv_heads, (((1,), (1,)), ((), ())), preferred_element_type=f32
        )
    )
    input_grad = (
        residual_grad
        + inv_first * scaled_in_grad
        - tokens * inv_first**3 * jnp.mean(scaled_in_grad * tokens, -1, keepdims=True)
    )

    grad_all = gather_rows(attn_grad)
    out_term = lax.dot_general(
        attended_rows, grad_all, (((0,), (0,)), ((), ())), preferred_element_type=f32
    ).astype(bf16)
    out_pieces = lax.all_to_all(
        out_term.reshape(n_fsdp, shard, MODEL_WIDTH), "fsdp", 0, 0, tiled=True
    )
    out_grad = jnp.sum(out_pieces.astype(f32), 0)
    qkv_term = lax.dot_general(
        unit_all, qkv_rows, (((0,), (0,)), ((), ())), preferred_element_type=f32
    ).astype(bf16)
    qkv_pieces = lax.all_to_all(
        qkv_term.reshape(n_all, shard, cols), both, 0, 0, tiled=True
    ).reshape(n_ctx, n_fsdp, shard, cols)
    qkv_sum = jnp.sum(qkv_pieces.astype(f32), 1)
    kv_sum = jnp.sum(
        qkv_sum[..., q_cols:].reshape(n_ctx // share, share, shard, 2, kv_cols), 1
    ).transpose(1, 2, 0, 3)
    unit_grad = jnp.concatenate(
        [
            qkv_sum[..., :q_cols].transpose(1, 0, 2).reshape(shard, QUERY_FEATURES),
            kv_sum.reshape(shard, 2 * KEY_FEATURES),
        ],
        1,
    )
    qkv_grad = gain_shard[0][:, None] * unit_grad
    gain_attn_grad = jnp.sum(qkv_shard * unit_grad, 1)
    gain_ffn_pieces = lax.all_to_all(
        gain_ffn_part.reshape(n_all, 1, shard), both, 0, 0, tiled=True
    )
    gain_ffn_grad = jnp.sum(gain_ffn_pieces, (0, 1))
    gains_grad = jnp.stack([gain_attn_grad, gain_ffn_grad])

    norm_new = adamw_update(norm_gains, gains_grad, norm_gains_first, norm_gains_second, 0.0)
    qkv_new = adamw_update(qkv_weight, qkv_grad, qkv_weight_first, qkv_weight_second, WEIGHT_DECAY)
    out_new = adamw_update(out_weight, out_grad, out_weight_first, out_weight_second, WEIGHT_DECAY)
    up_new = adamw_update(expert_up, up_grad_shard, expert_up_first, expert_up_second, WEIGHT_DECAY)
    down_new = adamw_update(
        expert_down, down_grad_shard, expert_down_first, expert_down_second, WEIGHT_DECAY
    )
    return (
        hidden_out[None],
        input_grad[None],
        gains_grad,
        qkv_grad,
        out_grad,
        up_grad_shard,
        down_grad_shard,
        norm_new[0],
        qkv_new[0],
        out_new[0],
        up_new[0],
        down_new[0],
        norm_new[1],
        qkv_new[1],
        out_new[1],
        up_new[1],
        down_new[1],
        norm_new[2],
        qkv_new[2],
        out_new[2],
        up_new[2],
        down_new[2],
    )


def solution(mesh):
    in_specs = (
        P("fsdp", "ctx", None),
        P("fsdp", "ctx", None),
        P("fsdp", "ctx", None),
        P("fsdp", "ctx", None),
        P(None, ("ctx", "fsdp")),
        P(("ctx", "fsdp"), None),
        P(("ctx", "fsdp"), None),
        P("ctx", "fsdp", None),
        P("ctx", None, "fsdp"),
        P(None, ("ctx", "fsdp")),
        P(("ctx", "fsdp"), None),
        P(("ctx", "fsdp"), None),
        P("ctx", "fsdp", None),
        P("ctx", None, "fsdp"),
        P(None, ("ctx", "fsdp")),
        P(("ctx", "fsdp"), None),
        P(("ctx", "fsdp"), None),
        P("ctx", "fsdp", None),
        P("ctx", None, "fsdp"),
    )
    out_specs = (
        P("fsdp", "ctx", None),
        P("fsdp", "ctx", None),
        P(None, ("ctx", "fsdp")),
        P(("ctx", "fsdp"), None),
        P(("ctx", "fsdp"), None),
        P("ctx", "fsdp", None),
        P("ctx", None, "fsdp"),
        P(None, ("ctx", "fsdp")),
        P(("ctx", "fsdp"), None),
        P(("ctx", "fsdp"), None),
        P("ctx", "fsdp", None),
        P("ctx", None, "fsdp"),
        P(None, ("ctx", "fsdp")),
        P(("ctx", "fsdp"), None),
        P(("ctx", "fsdp"), None),
        P("ctx", "fsdp", None),
        P("ctx", None, "fsdp"),
        P(None, ("ctx", "fsdp")),
        P(("ctx", "fsdp"), None),
        P(("ctx", "fsdp"), None),
        P("ctx", "fsdp", None),
        P("ctx", None, "fsdp"),
    )
    return jax.shard_map(local, mesh=mesh, in_specs=in_specs, out_specs=out_specs, check_vma=False)
```

```python
import jax
import jax.numpy as jnp
from jax import lax
from jax.experimental import pallas as pl
from jax.experimental.layout import Layout, with_layout_constraint
from jax.experimental.pallas import tpu as pltpu
from jax.sharding import PartitionSpec as P

MODEL_WIDTH = 1024
QUERY_HEADS = 16
KEY_VALUE_HEADS = 8
HEAD_SIZE = 64
FF = 512
TOP = 8
DEVICE_TOKENS = 128
QUERY_FEATURES = 1024
KEY_FEATURES = 512


RES_SCALE = 0.22
SCORE_SCALE = 0.015625
NORM_EPS = 1e-06
ROPE_BASE = 10000.0
LEARN_RATE = 0.02
BETA_FIRST = 0.9
BETA_SECOND = 0.999
ADAM_EPS = 1e-08
WEIGHT_DECAY = 0.1
ADAM_STEP = 3.0
MASK_VALUE = -1e30


def positions(row_ids, tok_dev, n_ctx):
    device = row_ids // tok_dev
    within = row_ids % tok_dev
    half_block = tok_dev // 2
    return jnp.where(
        within < half_block,
        device * half_block + within,
        (2 * n_ctx - 1 - device) * half_block + within - half_block,
    )


def rope_tables(position, head_dim):
    half_dim = head_dim // 2
    frequency = ROPE_BASE ** (-(jnp.arange(half_dim, dtype=jnp.float32) * 2.0 / head_dim))
    angles = position.astype(jnp.float32)[:, None] * frequency[None, :]
    return (jnp.cos(angles)[:, None, :], jnp.sin(angles)[:, None, :])


def apply_rotary(values, cosine_table, sine_table):
    half_dim = values.shape[-1] // 2
    lower_half, upper_half = (values[..., :half_dim], values[..., half_dim:])
    return jnp.concatenate(
        [
            lower_half * cosine_table - upper_half * sine_table,
            upper_half * cosine_table + lower_half * sine_table,
        ],
        -1,
    )


def inverse_rotary(cotangent, cosine_table, sine_table):
    half_dim = cotangent.shape[-1] // 2
    lower_half, upper_half = (cotangent[..., :half_dim], cotangent[..., half_dim:])
    return jnp.concatenate(
        [
            lower_half * cosine_table + upper_half * sine_table,
            upper_half * cosine_table - lower_half * sine_table,
        ],
        -1,
    )


def scores_of(queries, key_head_rows, q_pos, k_pos):
    raw_scores = jnp.einsum(
        "qgrd,kgd->grqk", queries, key_head_rows, preferred_element_type=jnp.float32
    )
    raw_scores = raw_scores * SCORE_SCALE
    allowed = k_pos[None, :] <= q_pos[:, None]
    return jnp.where(allowed, raw_scores, MASK_VALUE)


def attend(queries, key_head_rows, value_head_rows, q_pos, k_pos):
    scores = scores_of(queries, key_head_rows, q_pos, k_pos)
    row_max = jnp.max(scores, -1, keepdims=True)
    logarithm_total = row_max + jnp.log(jnp.sum(jnp.exp(scores - row_max), -1, keepdims=True))
    attn_probs = jnp.exp(scores - logarithm_total).astype(jnp.bfloat16)
    output = jnp.einsum(
        "grqk,kgd->qgrd", attn_probs, value_head_rows, preferred_element_type=jnp.float32
    ).astype(jnp.bfloat16)
    return (output, logarithm_total)


def attend_back(
    queries, key_head_rows, value_head_rows, output, out_grad, logarithm_total, q_pos, k_pos
):
    scores = scores_of(queries, key_head_rows, q_pos, k_pos)
    attn_probs = jnp.exp(scores - logarithm_total)
    value_gradient = jnp.einsum(
        "grqk,qgrd->kgd",
        attn_probs.astype(jnp.bfloat16),
        out_grad,
        preferred_element_type=jnp.float32,
    )
    prob_grad = jnp.einsum(
        "qgrd,kgd->grqk", out_grad, value_head_rows, preferred_element_type=jnp.float32
    )
    row_dot = jnp.einsum("qgrd,qgrd->grq", out_grad, output, preferred_element_type=jnp.float32)[
        ..., None
    ]
    score_grad = (attn_probs * (prob_grad - row_dot) * SCORE_SCALE).astype(jnp.bfloat16)
    query_gradient = jnp.einsum(
        "grqk,kgd->qgrd", score_grad, key_head_rows, preferred_element_type=jnp.float32
    )
    key_gradient = jnp.einsum(
        "grqk,qgrd->kgd", score_grad, queries, preferred_element_type=jnp.float32
    )
    return (query_gradient, key_gradient, value_gradient)


def adamw_update(weight, gradient, first_moment, second_moment, decay_rate):
    first_new = BETA_FIRST * first_moment + (1.0 - BETA_FIRST) * gradient
    second_new = BETA_SECOND * second_moment + (1.0 - BETA_SECOND) * gradient * gradient
    first_hat = first_new / (1.0 - BETA_FIRST**ADAM_STEP)
    second_hat = second_new / (1.0 - BETA_SECOND**ADAM_STEP)
    weight_new = weight - LEARN_RATE * (
        first_hat / (jnp.sqrt(second_hat) + ADAM_EPS) + decay_rate * weight
    )
    return (weight_new, first_new, second_new)


def xor_perm(size, mask):
    return [(i, i ^ mask) for i in range(size)]


def exchange(values, axis, mask):
    return lax.ppermute(values, axis, xor_perm(lax.axis_size(axis), mask))


def relative_order(size):
    return list(range(0, size, 2)) + list(range(1, size, 2))


def assemble(pieces, spans):
    count = len(pieces)
    order = relative_order(count)

    def body(index_ref, *refs):
        outs = refs[count : count + len(spans)]
        copies = []
        for place in range(count):
            for number, (start, length, natural) in enumerate(spans):
                at = place * length
                if natural:
                    at = pl.multiple_of((index_ref[0] ^ order[place]) * length, length)
                copies.append(
                    pltpu.make_async_copy(
                        refs[place].at[pl.ds(start, length)],
                        outs[number].at[pl.ds(at, length)],
                        refs[-1].at[place, number],
                    )
                )
        for copy in copies:
            copy.start()
        for copy in copies:
            copy.wait()

    width = pieces[0].shape[1]
    return pl.pallas_call(
        body,
        out_shape=[
            jax.ShapeDtypeStruct((count * span[1], width), pieces[0].dtype) for span in spans
        ],
        in_specs=[pl.BlockSpec(memory_space=pltpu.SMEM)]
        + [pl.BlockSpec(memory_space=pl.ANY)] * count,
        out_specs=[pl.BlockSpec(memory_space=pltpu.VMEM)] * len(spans),
        scratch_shapes=[pltpu.SemaphoreType.DMA((count, len(spans)))],
        name="assemble",
    )(device_index("ctx"), *pieces)


def device_index(axis):
    return lax.axis_index(axis).astype(jnp.int32).reshape(1)


def reorder(rows, count, to_natural):
    length = rows.shape[0] // count
    order = relative_order(count)

    def body(index_ref, rows_ref, out_ref):
        for place in range(count):
            there = pl.ds(pl.multiple_of((index_ref[0] ^ order[place]) * length, length), length)
            here = pl.ds(place * length, length)
            if to_natural:
                out_ref[there, :] = rows_ref[here, :]
            else:
                out_ref[here, :] = rows_ref[there, :]

    return pl.pallas_call(
        body,
        out_shape=jax.ShapeDtypeStruct(rows.shape, rows.dtype),
        in_specs=[
            pl.BlockSpec(memory_space=pltpu.SMEM),
            pl.BlockSpec(memory_space=pltpu.VMEM),
        ],
        out_specs=pl.BlockSpec(memory_space=pltpu.VMEM),
        name="reorder",
    )(device_index("ctx"), rows)


def project_out(heads, out_all, tokens, gain):
    count = heads.shape[0] // tokens.shape[0]
    length, width = tokens.shape
    cols = heads.shape[1]

    def body(heads_ref, out_ref, tokens_ref, gain_ref, residual_ref, normed_ref):
        total = jnp.zeros((length, width), jnp.float32)
        for place in range(count):
            total = total + jnp.dot(
                heads_ref[place * length : (place + 1) * length, :],
                out_ref[place * cols : (place + 1) * cols, :],
                preferred_element_type=jnp.float32,
            )
        residual = tokens_ref[...] + RES_SCALE * total
        inv = lax.rsqrt(jnp.mean(residual * residual, -1, keepdims=True) + NORM_EPS)
        residual_ref[...] = residual
        normed_ref[...] = (residual * inv * gain_ref[...]).astype(jnp.bfloat16)

    vmem = pl.BlockSpec(memory_space=pltpu.VMEM)
    return pl.pallas_call(
        body,
        out_shape=[
            jax.ShapeDtypeStruct((length, width), jnp.float32),
            jax.ShapeDtypeStruct((length, width), jnp.bfloat16),
        ],
        in_specs=[vmem] * 4,
        out_specs=[vmem] * 2,
        name="project_out",
    )(heads, out_all, tokens, gain)


def residual_back(own, received, residual, cotangent, gain, out_all):
    length, width = residual.shape
    count = lax.axis_size("ctx")
    cols = out_all.shape[0] // count
    n_parts = len(received)

    def body(own_ref, *refs):
        parts = refs[:n_parts]
        residual_ref, cotangent_ref, gain_ref, out_ref = refs[n_parts : n_parts + 4]
        grad_ref, attn_ref, gain_grad_ref, heads_ref = refs[n_parts + 4 :]
        ffn_grad = own_ref[...]
        for part in parts:
            ffn_grad = ffn_grad + part[...].astype(jnp.float32)
        rows = residual_ref[...]
        inv = lax.rsqrt(jnp.mean(rows * rows, -1, keepdims=True) + NORM_EPS)
        weighted = gain_ref[...] * ffn_grad
        gain_grad_ref[...] = jnp.sum(ffn_grad * rows * inv, 0, keepdims=True)
        grad = (
            cotangent_ref[...]
            + inv * weighted
            - rows * (inv * inv * inv) * jnp.mean(weighted * rows, -1, keepdims=True)
        )
        grad_ref[...] = grad
        attn_grad = (RES_SCALE * grad).astype(jnp.bfloat16)
        attn_ref[...] = attn_grad
        for place in range(count):
            heads_ref[place * length : (place + 1) * length, :] = lax.dot_general(
                attn_grad,
                out_ref[place * cols : (place + 1) * cols, :],
                (((1,), (1,)), ((), ())),
                preferred_element_type=jnp.float32,
            ).astype(jnp.bfloat16)

    vmem = pl.BlockSpec(memory_space=pltpu.VMEM)
    return pl.pallas_call(
        body,
        out_shape=[
            jax.ShapeDtypeStruct((length, width), jnp.float32),
            jax.ShapeDtypeStruct((length, width), jnp.bfloat16),
            jax.ShapeDtypeStruct((1, width), jnp.float32),
            jax.ShapeDtypeStruct((count * length, cols), jnp.bfloat16),
        ],
        in_specs=[vmem] * (5 + n_parts),
        out_specs=[vmem] * 4,
        name="residual_back",
    )(own, *received, residual, cotangent, gain, out_all)


def row_pieces(rows):
    size = lax.axis_size("ctx")
    even = [rows] + [exchange(rows, "ctx", mask) for mask in range(2, size, 2)]
    return even + [exchange(piece, "ctx", 1) for piece in even]


def gather_rows(rows):
    return assemble(row_pieces(rows), [(0, rows.shape[0], False)])[0]


def gather_down(shard):
    size = lax.axis_size("fsdp")
    pieces = [shard] + [exchange(shard, "fsdp", mask) for mask in range(1, size)]
    count, hidden, width = shard.shape

    def body(index_ref, *refs):
        copies = []
        for mask in range(size):
            place = pl.multiple_of((index_ref[0] ^ mask) * width, width)
            copies.append(
                pltpu.make_async_copy(
                    refs[mask], refs[size].at[:, :, pl.ds(place, width)], refs[-1].at[mask]
                )
            )
        for copy in copies:
            copy.start()
        for copy in copies:
            copy.wait()

    return pl.pallas_call(
        body,
        out_shape=jax.ShapeDtypeStruct((count, hidden, size * width), shard.dtype),
        in_specs=[pl.BlockSpec(memory_space=pltpu.SMEM)]
        + [pl.BlockSpec(memory_space=pl.ANY)] * size,
        out_specs=pl.BlockSpec(memory_space=pltpu.VMEM),
        scratch_shapes=[pltpu.SemaphoreType.DMA((size,))],
        name="assemble_down",
    )(device_index("fsdp"), *pieces)


def scatter_parts(even_rows, odd_rows):
    size = lax.axis_size("ctx")
    block = even_rows.shape[0] * 2 // size
    other = exchange(odd_rows, "ctx", 1)
    pair_sum = even_rows + other.astype(jnp.float32)
    received = []
    for place in range(1, size // 2):
        piece = pair_sum[place * block : (place + 1) * block].astype(jnp.bfloat16)
        received.append(exchange(piece, "ctx", 2 * place))
    return pair_sum[:block], received


def scatter_sum(even_rows, odd_rows):
    total, received = scatter_parts(even_rows, odd_rows)
    for part in received:
        total = total + part.astype(jnp.float32)
    return total


def expert_front(pieces, up_work, down_back, weight_own):
    count = len(pieces)
    tokens, width = pieces[0].shape
    seq = count * tokens
    n_exp = up_work.shape[0]
    step = 256
    steps = seq // step
    half = steps // 2

    def body(*refs):
        up_ref, back_ref, weight_ref = refs[count : count + 3]
        rows_ref, hidden_ref, pair_ref, even_ref, odd_ref, sems = refs[count + 3 :]
        number = pl.program_id(0)

        @pl.when(number == 0)
        def _():
            copies = [
                pltpu.make_async_copy(
                    refs[k], rows_ref.at[pl.ds(k * tokens, tokens)], sems.at[k]
                )
                for k in range(count)
            ]
            for copy in copies:
                copy.start()
            for copy in copies:
                copy.wait()

        rows = rows_ref[pl.ds(pl.multiple_of(number * step, step), step), :]
        total = jnp.zeros((step, width), jnp.float32)
        for e in range(n_exp):
            gate_up = jnp.dot(rows, up_ref[e], preferred_element_type=jnp.float32)
            gate = gate_up[:, :FF]
            up = gate_up[:, FF:]
            sig = 1.0 / (1.0 + jnp.exp(-gate))
            weight = weight_ref[:, e : e + 1]
            act = gate * sig
            hidden_ref[:, e * FF : (e + 1) * FF] = (weight * (act * up)).astype(jnp.bfloat16)
            back = weight * back_ref[:, e * FF : (e + 1) * FF]
            first = back * up * sig * (1.0 + gate * (1.0 - sig))
            pair = jnp.concatenate([first, back * act], 1).astype(jnp.bfloat16)
            pair_ref[e] = pair
            total = total + lax.dot_general(
                pair, up_ref[e], (((1,), (1,)), ((), ())), preferred_element_type=jnp.float32
            )

        @pl.when(number < half)
        def _():
            even_ref[...] = total

        @pl.when(number >= half)
        def _():
            odd_ref[...] = total.astype(jnp.bfloat16)

    return pl.pallas_call(
        body,
        grid=(steps,),
        out_shape=[
            jax.ShapeDtypeStruct((seq, width), jnp.bfloat16),
            jax.ShapeDtypeStruct((seq, n_exp * FF), jnp.bfloat16),
            jax.ShapeDtypeStruct((n_exp, seq, 2 * FF), jnp.bfloat16),
            jax.ShapeDtypeStruct((seq // 2, width), jnp.float32),
            jax.ShapeDtypeStruct((seq // 2, width), jnp.bfloat16),
        ],
        in_specs=[pl.BlockSpec(memory_space=pl.ANY)] * count
        + [
            pl.BlockSpec(up_work.shape, lambda i: (0, 0, 0)),
            pl.BlockSpec((step, n_exp * FF), lambda i: (i, 0)),
            pl.BlockSpec((step, n_exp), lambda i: (i, 0)),
        ],
        out_specs=[
            pl.BlockSpec((seq, width), lambda i: (0, 0)),
            pl.BlockSpec((step, n_exp * FF), lambda i: (i, 0)),
            pl.BlockSpec((n_exp, step, 2 * FF), lambda i: (0, i, 0)),
            pl.BlockSpec((step, width), lambda i: (jnp.minimum(i, half - 1), 0)),
            pl.BlockSpec((step, width), lambda i: (jnp.maximum(i - half, 0), 0)),
        ],
        scratch_shapes=[pltpu.SemaphoreType.DMA((count,))],
        compiler_params=pltpu.CompilerParams(vmem_limit_bytes=56 * 1024 * 1024),
        name="expert_front",
    )(*pieces, up_work, down_back, weight_own)


def local(
    hidden_in,
    out_cotangent,
    routes,
    route_probs,
    norm_gains,
    qkv_weight,
    out_weight,
    expert_up,
    expert_down,
    norm_gains_first,
    qkv_weight_first,
    out_weight_first,
    expert_up_first,
    expert_down_first,
    norm_gains_second,
    qkv_weight_second,
    out_weight_second,
    expert_up_second,
    expert_down_second,
):
    f32 = jnp.float32
    bf16 = jnp.bfloat16
    both = ("ctx", "fsdp")
    n_ctx = lax.axis_size("ctx")
    n_fsdp = lax.axis_size("fsdp")
    n_all = n_ctx * n_fsdp
    ctx_index = lax.axis_index("ctx")
    n_exp = expert_up.shape[0]
    shard = qkv_weight.shape[0]
    seq = DEVICE_TOKENS * n_ctx
    q_dev = QUERY_HEADS // n_ctx
    kv_dev = max(1, KEY_VALUE_HEADS // n_ctx)
    share = max(1, n_ctx // KEY_VALUE_HEADS)
    q_cols = q_dev * HEAD_SIZE
    kv_cols = kv_dev * HEAD_SIZE
    cols = q_cols + 2 * kv_cols

    tokens = hidden_in[0]
    cotangent = out_cotangent[0]
    inv_first = lax.rsqrt(jnp.mean(tokens * tokens, -1, keepdims=True) + NORM_EPS)
    unit_rows = (tokens * inv_first).astype(bf16)
    unit_all = gather_rows(unit_rows)

    gain_shard = norm_gains.astype(bf16).astype(f32)
    qkv_shard = qkv_weight.astype(bf16).astype(f32)
    scaled = (qkv_shard * gain_shard[0][:, None]).astype(bf16)
    q_part = scaled[:, :QUERY_FEATURES].reshape(shard, n_ctx, q_cols)
    k_part = scaled[:, QUERY_FEATURES : QUERY_FEATURES + KEY_FEATURES]
    v_part = scaled[:, QUERY_FEATURES + KEY_FEATURES :]
    k_part = jnp.repeat(k_part.reshape(shard, n_ctx // share, kv_cols), share, 1)
    v_part = jnp.repeat(v_part.reshape(shard, n_ctx // share, kv_cols), share, 1)
    head_cols = jnp.concatenate([q_part, k_part, v_part], -1).transpose(1, 0, 2)
    head_cols = jnp.broadcast_to(head_cols[:, None], (n_ctx, n_fsdp, shard, cols))
    qkv_heads = lax.all_to_all(
        head_cols.reshape(n_all, shard, cols), both, split_axis=0, concat_axis=0, tiled=True
    ).reshape(MODEL_WIDTH, cols)

    up_work = lax.all_gather(expert_up.astype(bf16), "fsdp", axis=1, tiled=True)
    gain_row = jnp.pad(norm_gains[1:2].astype(bf16), ((0, 7), (0, MODEL_WIDTH - shard)))
    out_shard = jnp.concatenate([out_weight.astype(bf16), gain_row], 0)
    out_group = lax.all_to_all(
        jnp.broadcast_to(out_shard[None], (n_fsdp,) + out_shard.shape), "fsdp", 0, 0, tiled=True
    )
    down_shard, out_group = lax.optimization_barrier((expert_down.astype(bf16), out_group))
    down_work = gather_down(down_shard)
    experts = jnp.arange(n_exp * n_ctx, dtype=jnp.int32)
    chosen = routes[0][:, None, :] == experts[None, :, None]
    weight_rows = jnp.sum(jnp.where(chosen, route_probs[0][:, None, :], 0.0), 2).T
    weight_high = lax.reduce_precision(weight_rows, 8, 7)
    weight_low = weight_rows - weight_high
    weight_flat = jnp.stack([weight_high, weight_low]).reshape(-1, MODEL_WIDTH).astype(bf16)
    gain_flat = out_group[:, shard, :shard].reshape(1, n_fsdp * shard)
    gain_flat = jnp.pad(gain_flat, ((0, 0), (0, MODEL_WIDTH - n_fsdp * shard)))
    n_misc = weight_flat.shape[0]
    misc_rows = -(-(n_misc + 1) // 16) * 16
    payload = jnp.concatenate(
        [
            (RES_SCALE * cotangent).astype(bf16),
            out_group[:, :shard].reshape(q_cols, MODEL_WIDTH),
            weight_flat,
            gain_flat,
            jnp.zeros((misc_rows - n_misc - 1, MODEL_WIDTH), bf16),
        ],
        0,
    )
    cotangent_all, out_all, misc_all = assemble(
        row_pieces(payload),
        [
            (0, DEVICE_TOKENS, False),
            (DEVICE_TOKENS, q_cols, True),
            (DEVICE_TOKENS + q_cols, misc_rows, False),
        ],
    )
    misc_all = misc_all.reshape(n_ctx, misc_rows, MODEL_WIDTH)
    weight_all = (
        misc_all[:, :n_misc]
        .astype(f32)
        .reshape(n_ctx, 2, n_exp * n_ctx, DEVICE_TOKENS)
    )
    weight_all = lax.dynamic_slice_in_dim(
        weight_all[:, 0] + weight_all[:, 1], ctx_index * n_exp, n_exp, 1
    )
    weight_own = weight_all.transpose(0, 2, 1).reshape(seq, n_exp)
    device_ids = ctx_index ^ jnp.array(relative_order(n_ctx), jnp.int32)
    gain_pieces = misc_all[:, n_misc, : n_fsdp * shard].astype(f32)
    is_piece = device_ids[None, :] == jnp.arange(n_ctx, dtype=jnp.int32)[:, None]
    gain_ffn = jnp.sum(jnp.where(is_piece[:, :, None], gain_pieces[None], 0.0), 1).reshape(
        1, MODEL_WIDTH
    )

    row_ids = device_ids[:, None] * DEVICE_TOKENS + jnp.arange(DEVICE_TOKENS, dtype=jnp.int32)
    position = positions(row_ids.reshape(-1), DEVICE_TOKENS, n_ctx)
    cosine_table, sine_table = rope_tables(position, HEAD_SIZE)

    projected = jnp.dot(unit_all, qkv_heads, preferred_element_type=f32)
    query_heads = (
        apply_rotary(
            projected[:, :q_cols].reshape(seq, q_dev, HEAD_SIZE), cosine_table, sine_table
        )
        .astype(bf16)
        .reshape(seq, kv_dev, q_dev // kv_dev, HEAD_SIZE)
    )
    key_heads = apply_rotary(
        projected[:, q_cols : q_cols + kv_cols].reshape(seq, kv_dev, HEAD_SIZE),
        cosine_table,
        sine_table,
    ).astype(bf16)
    value_heads = projected[:, q_cols + kv_cols :].astype(bf16).reshape(seq, kv_dev, HEAD_SIZE)
    attended, logarithm_total = attend(query_heads, key_heads, value_heads, position, position)
    attended_rows = attended.reshape(seq, q_cols)
    attended_natural = reorder(attended_rows, n_ctx, True)
    attn_rows = lax.all_to_all(attended_natural, "ctx", 0, 0, tiled=True)
    residual, normed_ffn = project_out(attn_rows, out_all, tokens, gain_ffn)

    down_flat = down_work.reshape(n_exp * FF, MODEL_WIDTH)
    down_back = lax.dot_general(
        cotangent_all, down_flat, (((1,), (1,)), ((), ())), preferred_element_type=f32
    )
    normed_all, weighted_hidden, pair_grad, even_input, odd_input = expert_front(
        row_pieces(normed_ffn), up_work, down_back, weight_own
    )
    half = seq // 2
    own_grad, other_grads = scatter_parts(even_input, odd_input)
    up_term = jnp.einsum(
        "md,emf->edf", normed_all, pair_grad, preferred_element_type=f32
    ).astype(bf16)
    up_term = with_layout_constraint(up_term, Layout(major_to_minor=(0, 1, 2)))
    up_grad_shard = lax.psum_scatter(up_term, "fsdp", scatter_dimension=1, tiled=True).astype(f32)
    down_term = lax.dot_general(
        weighted_hidden, cotangent_all, (((0,), (0,)), ((), ())), preferred_element_type=f32
    ).astype(bf16)
    down_width = MODEL_WIDTH // n_fsdp
    fsdp_index = lax.axis_index("fsdp")

    def down_block(mask):
        return lax.dynamic_slice_in_dim(down_term, (fsdp_index ^ mask) * down_width, down_width, 1)

    down_parts = [down_block(0)] + [
        exchange(down_block(mask), "fsdp", mask) for mask in range(1, n_fsdp)
    ]

    def value_rows(rows):
        return jnp.dot(rows, down_flat, preferred_element_type=f32)

    odd_value = value_rows(weighted_hidden[half:]).astype(bf16)
    hidden_out = residual + RES_SCALE * scatter_sum(value_rows(weighted_hidden[:half]), odd_value)

    residual_grad, attn_grad, gain_ffn_part, head_grads = residual_back(
        own_grad, other_grads, residual, cotangent, gain_ffn, out_all
    )
    gain_ffn_part = gain_ffn_part[0]
    attn_out_heads = reorder(
        lax.all_to_all(head_grads, "ctx", 0, 0, tiled=True), n_ctx, False
    )
    query_gradient, key_gradient, value_gradient = attend_back(
        query_heads,
        key_heads,
        value_heads,
        attended,
        attn_out_heads.reshape(seq, kv_dev, q_dev // kv_dev, HEAD_SIZE),
        logarithm_total,
        position,
        position,
    )
    query_rows = inverse_rotary(
        query_gradient.reshape(seq, q_dev, HEAD_SIZE), cosine_table, sine_table
    )
    key_rows = inverse_rotary(key_gradient, cosine_table, sine_table)
    qkv_rows = jnp.concatenate(
        [
            query_rows.reshape(seq, q_cols),
            key_rows.reshape(seq, kv_cols),
            value_gradient.reshape(seq, kv_cols),
        ],
        1,
    ).astype(bf16)

    def in_grad_rows(rows):
        return lax.dot_general(
            rows, qkv_heads, (((1,), (1,)), ((), ())), preferred_element_type=f32
        )

    odd_in_grad = in_grad_rows(qkv_rows[half:]).astype(bf16)
    scaled_in_grad = scatter_sum(in_grad_rows(qkv_rows[:half]), odd_in_grad)
    scaled_in_grad, down_parts = lax.optimization_barrier((scaled_in_grad, down_parts))
    down_grad = down_parts[0].astype(f32)
    for part in down_parts[1:]:
        down_grad = down_grad + part.astype(f32)
    down_grad_shard = down_grad.reshape(n_exp, FF, down_width)
    input_grad = (
        residual_grad
        + inv_first * scaled_in_grad
        - tokens * inv_first**3 * jnp.mean(scaled_in_grad * tokens, -1, keepdims=True)
    )

    grad_all = gather_rows(attn_grad)
    out_term = lax.dot_general(
        attended_rows, grad_all, (((0,), (0,)), ((), ())), preferred_element_type=f32
    ).astype(bf16)
    out_pieces = lax.all_to_all(
        out_term.reshape(n_fsdp, shard, MODEL_WIDTH), "fsdp", 0, 0, tiled=True
    )
    out_grad = jnp.sum(out_pieces.astype(f32), 0)
    qkv_term = lax.dot_general(
        unit_all, qkv_rows, (((0,), (0,)), ((), ())), preferred_element_type=f32
    ).astype(bf16)
    gain_high = lax.reduce_precision(gain_ffn_part, 8, 7)
    gain_parts = jnp.stack([gain_high, gain_ffn_part - gain_high]).reshape(2, n_all, shard)
    gain_parts = jnp.pad(
        gain_parts.transpose(1, 0, 2).astype(bf16), ((0, 0), (0, 6), (0, cols - shard))
    )
    qkv_pieces = lax.all_to_all(
        jnp.concatenate([qkv_term.reshape(n_all, shard, cols), gain_parts], 1),
        both,
        0,
        0,
        tiled=True,
    ).reshape(n_ctx, n_fsdp, shard + 8, cols)
    gain_ffn_grad = jnp.sum(qkv_pieces[:, :, shard : shard + 2, :shard].astype(f32), (0, 1, 2))
    qkv_pieces = qkv_pieces[:, :, :shard]
    qkv_sum = jnp.sum(qkv_pieces.astype(f32), 1)
    kv_sum = jnp.sum(
        qkv_sum[..., q_cols:].reshape(n_ctx // share, share, shard, 2, kv_cols), 1
    ).transpose(1, 2, 0, 3)
    unit_grad = jnp.concatenate(
        [
            qkv_sum[..., :q_cols].transpose(1, 0, 2).reshape(shard, QUERY_FEATURES),
            kv_sum.reshape(shard, 2 * KEY_FEATURES),
        ],
        1,
    )
    qkv_grad = gain_shard[0][:, None] * unit_grad
    gain_attn_grad = jnp.sum(qkv_shard * unit_grad, 1)
    gains_grad = jnp.stack([gain_attn_grad, gain_ffn_grad])

    norm_new = adamw_update(norm_gains, gains_grad, norm_gains_first, norm_gains_second, 0.0)
    qkv_new = adamw_update(qkv_weight, qkv_grad, qkv_weight_first, qkv_weight_second, WEIGHT_DECAY)
    out_new = adamw_update(out_weight, out_grad, out_weight_first, out_weight_second, WEIGHT_DECAY)
    up_new = adamw_update(expert_up, up_grad_shard, expert_up_first, expert_up_second, WEIGHT_DECAY)
    down_new = adamw_update(
        expert_down, down_grad_shard, expert_down_first, expert_down_second, WEIGHT_DECAY
    )
    return (
        hidden_out[None],
        input_grad[None],
        gains_grad,
        qkv_grad,
        out_grad,
        up_grad_shard,
        down_grad_shard,
        norm_new[0],
        qkv_new[0],
        out_new[0],
        up_new[0],
        down_new[0],
        norm_new[1],
        qkv_new[1],
        out_new[1],
        up_new[1],
        down_new[1],
        norm_new[2],
        qkv_new[2],
        out_new[2],
        up_new[2],
        down_new[2],
    )


def solution(mesh):
    in_specs = (
        P("fsdp", "ctx", None),
        P("fsdp", "ctx", None),
        P("fsdp", "ctx", None),
        P("fsdp", "ctx", None),
        P(None, ("ctx", "fsdp")),
        P(("ctx", "fsdp"), None),
        P(("ctx", "fsdp"), None),
        P("ctx", "fsdp", None),
        P("ctx", None, "fsdp"),
        P(None, ("ctx", "fsdp")),
        P(("ctx", "fsdp"), None),
        P(("ctx", "fsdp"), None),
        P("ctx", "fsdp", None),
        P("ctx", None, "fsdp"),
        P(None, ("ctx", "fsdp")),
        P(("ctx", "fsdp"), None),
        P(("ctx", "fsdp"), None),
        P("ctx", "fsdp", None),
        P("ctx", None, "fsdp"),
    )
    out_specs = (
        P("fsdp", "ctx", None),
        P("fsdp", "ctx", None),
        P(None, ("ctx", "fsdp")),
        P(("ctx", "fsdp"), None),
        P(("ctx", "fsdp"), None),
        P("ctx", "fsdp", None),
        P("ctx", None, "fsdp"),
        P(None, ("ctx", "fsdp")),
        P(("ctx", "fsdp"), None),
        P(("ctx", "fsdp"), None),
        P("ctx", "fsdp", None),
        P("ctx", None, "fsdp"),
        P(None, ("ctx", "fsdp")),
        P(("ctx", "fsdp"), None),
        P(("ctx", "fsdp"), None),
        P("ctx", "fsdp", None),
        P("ctx", None, "fsdp"),
        P(None, ("ctx", "fsdp")),
        P(("ctx", "fsdp"), None),
        P(("ctx", "fsdp"), None),
        P("ctx", "fsdp", None),
        P("ctx", None, "fsdp"),
    )
    return jax.shard_map(local, mesh=mesh, in_specs=in_specs, out_specs=out_specs, check_vma=False)
```

```python
import jax
import jax.numpy as jnp
from jax import lax
from jax.experimental import pallas as pl
from jax.experimental.layout import Layout, with_layout_constraint
from jax.experimental.pallas import tpu as pltpu
from jax.sharding import PartitionSpec as P

MODEL_WIDTH = 1024
QUERY_HEADS = 16
KEY_VALUE_HEADS = 8
HEAD_SIZE = 64
FF = 512
TOP = 8
DEVICE_TOKENS = 128
QUERY_FEATURES = 1024
KEY_FEATURES = 512


RES_SCALE = 0.22
SCORE_SCALE = 0.015625
NORM_EPS = 1e-06
ROPE_BASE = 10000.0
LEARN_RATE = 0.02
BETA_FIRST = 0.9
BETA_SECOND = 0.999
ADAM_EPS = 1e-08
WEIGHT_DECAY = 0.1
ADAM_STEP = 3.0
MASK_VALUE = -1e30
EXPERT_STEP = 512


def positions(row_ids, tok_dev, n_ctx):
    device = row_ids // tok_dev
    within = row_ids % tok_dev
    half_block = tok_dev // 2
    return jnp.where(
        within < half_block,
        device * half_block + within,
        (2 * n_ctx - 1 - device) * half_block + within - half_block,
    )


def rope_tables(position, head_dim):
    half_dim = head_dim // 2
    frequency = ROPE_BASE ** (-(jnp.arange(half_dim, dtype=jnp.float32) * 2.0 / head_dim))
    angles = position.astype(jnp.float32)[:, None] * frequency[None, :]
    return (jnp.cos(angles)[:, None, :], jnp.sin(angles)[:, None, :])


def apply_rotary(values, cosine_table, sine_table):
    half_dim = values.shape[-1] // 2
    lower_half, upper_half = (values[..., :half_dim], values[..., half_dim:])
    return jnp.concatenate(
        [
            lower_half * cosine_table - upper_half * sine_table,
            upper_half * cosine_table + lower_half * sine_table,
        ],
        -1,
    )


def inverse_rotary(cotangent, cosine_table, sine_table):
    half_dim = cotangent.shape[-1] // 2
    lower_half, upper_half = (cotangent[..., :half_dim], cotangent[..., half_dim:])
    return jnp.concatenate(
        [
            lower_half * cosine_table + upper_half * sine_table,
            upper_half * cosine_table - lower_half * sine_table,
        ],
        -1,
    )


def scores_of(queries, key_head_rows, q_pos, k_pos):
    raw_scores = jnp.einsum(
        "qgrd,kgd->grqk", queries, key_head_rows, preferred_element_type=jnp.float32
    )
    raw_scores = raw_scores * SCORE_SCALE
    allowed = k_pos[None, :] <= q_pos[:, None]
    return jnp.where(allowed, raw_scores, MASK_VALUE)


def attend(queries, key_head_rows, value_head_rows, q_pos, k_pos):
    scores = scores_of(queries, key_head_rows, q_pos, k_pos)
    row_max = jnp.max(scores, -1, keepdims=True)
    logarithm_total = row_max + jnp.log(jnp.sum(jnp.exp(scores - row_max), -1, keepdims=True))
    attn_probs = jnp.exp(scores - logarithm_total).astype(jnp.bfloat16)
    output = jnp.einsum(
        "grqk,kgd->qgrd", attn_probs, value_head_rows, preferred_element_type=jnp.float32
    ).astype(jnp.bfloat16)
    return (output, logarithm_total)


def attend_back(
    queries, key_head_rows, value_head_rows, output, out_grad, logarithm_total, q_pos, k_pos
):
    scores = scores_of(queries, key_head_rows, q_pos, k_pos)
    attn_probs = jnp.exp(scores - logarithm_total)
    value_gradient = jnp.einsum(
        "grqk,qgrd->kgd",
        attn_probs.astype(jnp.bfloat16),
        out_grad,
        preferred_element_type=jnp.float32,
    )
    prob_grad = jnp.einsum(
        "qgrd,kgd->grqk", out_grad, value_head_rows, preferred_element_type=jnp.float32
    )
    row_dot = jnp.einsum("qgrd,qgrd->grq", out_grad, output, preferred_element_type=jnp.float32)[
        ..., None
    ]
    score_grad = (attn_probs * (prob_grad - row_dot) * SCORE_SCALE).astype(jnp.bfloat16)
    query_gradient = jnp.einsum(
        "grqk,kgd->qgrd", score_grad, key_head_rows, preferred_element_type=jnp.float32
    )
    key_gradient = jnp.einsum(
        "grqk,qgrd->kgd", score_grad, queries, preferred_element_type=jnp.float32
    )
    return (query_gradient, key_gradient, value_gradient)


def adamw_update(weight, gradient, first_moment, second_moment, decay_rate):
    first_new = BETA_FIRST * first_moment + (1.0 - BETA_FIRST) * gradient
    second_new = BETA_SECOND * second_moment + (1.0 - BETA_SECOND) * gradient * gradient
    first_hat = first_new / (1.0 - BETA_FIRST**ADAM_STEP)
    second_hat = second_new / (1.0 - BETA_SECOND**ADAM_STEP)
    weight_new = weight - LEARN_RATE * (
        first_hat / (jnp.sqrt(second_hat) + ADAM_EPS) + decay_rate * weight
    )
    return (weight_new, first_new, second_new)


def xor_perm(size, mask):
    return [(i, i ^ mask) for i in range(size)]


def exchange(values, axis, mask):
    return lax.ppermute(values, axis, xor_perm(lax.axis_size(axis), mask))


def relative_order(size):
    return list(range(0, size, 2)) + list(range(1, size, 2))


def assemble(pieces, sizes, moves):
    count = len(pieces)
    order = relative_order(count)

    def body(index_ref, *refs):
        outs = refs[count : count + len(sizes)]
        copies = []
        for k in range(count):
            for m, (start, length, number, place) in enumerate(moves):
                at = place(k, order[k], index_ref[0], index_ref[1])
                if not isinstance(at, int):
                    at = pl.multiple_of(at, length)
                copies.append(
                    pltpu.make_async_copy(
                        refs[k].at[pl.ds(start, length)],
                        outs[number].at[pl.ds(at, length)],
                        refs[-1].at[k, m],
                    )
                )
        for copy in copies:
            copy.start()
        for copy in copies:
            copy.wait()

    width = pieces[0].shape[1]
    return pl.pallas_call(
        body,
        out_shape=[jax.ShapeDtypeStruct((size, width), pieces[0].dtype) for size in sizes],
        in_specs=[pl.BlockSpec(memory_space=pltpu.SMEM)]
        + [pl.BlockSpec(memory_space=pl.ANY)] * count,
        out_specs=[pl.BlockSpec(memory_space=pltpu.VMEM)] * len(sizes),
        scratch_shapes=[pltpu.SemaphoreType.DMA((count, len(moves)))],
        name="assemble",
    )(jnp.concatenate([device_index("ctx"), device_index("fsdp")]), *pieces)


def assemble_heads(pieces, shard):
    size = len(pieces)
    rows, cols = pieces[0].shape
    count = rows // shard

    def body(index_ref, *refs):
        copies = []
        for mask in range(size):
            for i in range(count):
                at = pl.multiple_of((i * size + (index_ref[0] ^ mask)) * shard, shard)
                copies.append(
                    pltpu.make_async_copy(
                        refs[mask].at[pl.ds(i * shard, shard)],
                        refs[size].at[pl.ds(at, shard)],
                        refs[-1].at[mask, i],
                    )
                )
        for copy in copies:
            copy.start()
        for copy in copies:
            copy.wait()

    return pl.pallas_call(
        body,
        out_shape=jax.ShapeDtypeStruct((rows * size, cols), pieces[0].dtype),
        in_specs=[pl.BlockSpec(memory_space=pltpu.SMEM)]
        + [pl.BlockSpec(memory_space=pl.ANY)] * size,
        out_specs=pl.BlockSpec(memory_space=pltpu.VMEM),
        scratch_shapes=[pltpu.SemaphoreType.DMA((size, count))],
        name="assemble_heads",
    )(device_index("fsdp"), *pieces)


def device_index(axis):
    return lax.axis_index(axis).astype(jnp.int32).reshape(1)


def reorder(rows, count, to_natural):
    length = rows.shape[0] // count
    order = relative_order(count)

    def body(index_ref, rows_ref, out_ref):
        for place in range(count):
            there = pl.ds(pl.multiple_of((index_ref[0] ^ order[place]) * length, length), length)
            here = pl.ds(place * length, length)
            if to_natural:
                out_ref[there, :] = rows_ref[here, :]
            else:
                out_ref[here, :] = rows_ref[there, :]

    return pl.pallas_call(
        body,
        out_shape=jax.ShapeDtypeStruct(rows.shape, rows.dtype),
        in_specs=[
            pl.BlockSpec(memory_space=pltpu.SMEM),
            pl.BlockSpec(memory_space=pltpu.VMEM),
        ],
        out_specs=pl.BlockSpec(memory_space=pltpu.VMEM),
        name="reorder",
    )(device_index("ctx"), rows)


def project_out(heads, out_all, tokens, gain):
    count = heads.shape[0] // tokens.shape[0]
    length, width = tokens.shape
    cols = heads.shape[1]

    def body(heads_ref, out_ref, tokens_ref, gain_ref, residual_ref, normed_ref):
        total = jnp.zeros((length, width), jnp.float32)
        for place in range(count):
            total = total + jnp.dot(
                heads_ref[place * length : (place + 1) * length, :],
                out_ref[place * cols : (place + 1) * cols, :],
                preferred_element_type=jnp.float32,
            )
        residual = tokens_ref[...] + RES_SCALE * total
        inv = lax.rsqrt(jnp.mean(residual * residual, -1, keepdims=True) + NORM_EPS)
        residual_ref[...] = residual
        normed_ref[...] = (residual * inv * gain_ref[...]).astype(jnp.bfloat16)

    vmem = pl.BlockSpec(memory_space=pltpu.VMEM)
    return pl.pallas_call(
        body,
        out_shape=[
            jax.ShapeDtypeStruct((length, width), jnp.float32),
            jax.ShapeDtypeStruct((length, width), jnp.bfloat16),
        ],
        in_specs=[vmem] * 4,
        out_specs=[vmem] * 2,
        name="project_out",
    )(heads, out_all, tokens, gain)


def residual_back(own, received, residual, cotangent, gain, out_all):
    length, width = residual.shape
    count = lax.axis_size("ctx")
    cols = out_all.shape[0] // count
    n_parts = len(received)

    def body(own_ref, *refs):
        parts = refs[:n_parts]
        residual_ref, cotangent_ref, gain_ref, out_ref = refs[n_parts : n_parts + 4]
        grad_ref, attn_ref, gain_grad_ref, heads_ref = refs[n_parts + 4 :]
        ffn_grad = own_ref[...]
        for part in parts:
            ffn_grad = ffn_grad + part[...].astype(jnp.float32)
        rows = residual_ref[...]
        inv = lax.rsqrt(jnp.mean(rows * rows, -1, keepdims=True) + NORM_EPS)
        weighted = gain_ref[...] * ffn_grad
        gain_grad_ref[...] = jnp.sum(ffn_grad * rows * inv, 0, keepdims=True)
        grad = (
            cotangent_ref[...]
            + inv * weighted
            - rows * (inv * inv * inv) * jnp.mean(weighted * rows, -1, keepdims=True)
        )
        grad_ref[...] = grad
        attn_grad = (RES_SCALE * grad).astype(jnp.bfloat16)
        attn_ref[...] = attn_grad
        for place in range(count):
            heads_ref[place * length : (place + 1) * length, :] = lax.dot_general(
                attn_grad,
                out_ref[place * cols : (place + 1) * cols, :],
                (((1,), (1,)), ((), ())),
                preferred_element_type=jnp.float32,
            ).astype(jnp.bfloat16)

    vmem = pl.BlockSpec(memory_space=pltpu.VMEM)
    return pl.pallas_call(
        body,
        out_shape=[
            jax.ShapeDtypeStruct((length, width), jnp.float32),
            jax.ShapeDtypeStruct((length, width), jnp.bfloat16),
            jax.ShapeDtypeStruct((1, width), jnp.float32),
            jax.ShapeDtypeStruct((count * length, cols), jnp.bfloat16),
        ],
        in_specs=[vmem] * (5 + n_parts),
        out_specs=[vmem] * 4,
        name="residual_back",
    )(own, *received, residual, cotangent, gain, out_all)


def row_pieces(rows):
    size = lax.axis_size("ctx")
    even = [rows] + [exchange(rows, "ctx", mask) for mask in range(2, size, 2)]
    return even + [exchange(piece, "ctx", 1) for piece in even]


def gather_rows(rows):
    length = rows.shape[0]
    pieces = row_pieces(rows)
    move = (0, length, 0, lambda k, mask, ctx, fsdp: k * length)
    return assemble(pieces, [length * len(pieces)], [move])[0]


def pair_parts(even_rows, odd_rows):
    size = lax.axis_size("ctx")
    block = even_rows.shape[0] * 2 // size
    pair_sum = even_rows + exchange(odd_rows, "ctx", 1).astype(jnp.float32)
    parts = [
        pair_sum[place * block : (place + 1) * block].astype(jnp.bfloat16)
        for place in range(1, size // 2)
    ]
    return pair_sum[:block], parts


def send_parts(parts):
    return [exchange(part, "ctx", 2 * place + 2) for place, part in enumerate(parts)]


def scatter_sum(even_rows, odd_rows):
    total, parts = pair_parts(even_rows, odd_rows)
    for part in send_parts(parts):
        total = total + part.astype(jnp.float32)
    return total


def expert_front(normed_all, cotangent_all, work, weight, before):
    seq, width = normed_all.shape
    step = EXPERT_STEP
    steps = seq // step
    half = steps // 2
    last = before is not None

    def body(rows_ref, back_ref, work_ref, weight_ref, *refs):
        if last:
            before_ref, hidden_ref, pair_ref, even_ref, odd_ref = refs
        else:
            hidden_ref, pair_ref, even_ref = refs
        gate_up = jnp.dot(rows_ref[...], work_ref[:, : 2 * FF], preferred_element_type=jnp.float32)
        gate = gate_up[:, :FF]
        up = gate_up[:, FF:]
        sig = 1.0 / (1.0 + jnp.exp(-gate))
        act = gate * sig
        hidden_ref[...] = (weight_ref[...] * (act * up)).astype(jnp.bfloat16)
        back = weight_ref[...] * jnp.dot(
            back_ref[...], work_ref[:, 2 * FF :], preferred_element_type=jnp.float32
        )
        pair_ref[:, :FF] = (back * up * sig * (1.0 + gate * (1.0 - sig))).astype(jnp.bfloat16)
        pair_ref[:, FF:] = (back * act).astype(jnp.bfloat16)
        total = lax.dot_general(
            pair_ref[...],
            work_ref[:, : 2 * FF],
            (((1,), (1,)), ((), ())),
            preferred_element_type=jnp.float32,
        )
        if not last:
            even_ref[...] = total
        else:
            total = total + before_ref[...]

            @pl.when(pl.program_id(0) < half)
            def _():
                even_ref[...] = total

            @pl.when(pl.program_id(0) >= half)
            def _():
                odd_ref[...] = total.astype(jnp.bfloat16)

    rows_spec = pl.BlockSpec((step, width), lambda i: (i, 0))
    out_shape = [
        jax.ShapeDtypeStruct((seq, FF), jnp.bfloat16),
        jax.ShapeDtypeStruct((seq, 2 * FF), jnp.bfloat16),
    ]
    out_specs = [
        pl.BlockSpec((step, FF), lambda i: (i, 0)),
        pl.BlockSpec((step, 2 * FF), lambda i: (i, 0)),
    ]
    if last:
        out_shape += [
            jax.ShapeDtypeStruct((seq // 2, width), jnp.float32),
            jax.ShapeDtypeStruct((seq // 2, width), jnp.bfloat16),
        ]
        out_specs += [
            pl.BlockSpec((step, width), lambda i: (jnp.minimum(i, half - 1), 0)),
            pl.BlockSpec((step, width), lambda i: (jnp.maximum(i - half, 0), 0)),
        ]
    else:
        out_shape.append(jax.ShapeDtypeStruct((seq, width), jnp.float32))
        out_specs.append(rows_spec)
    return pl.pallas_call(
        body,
        grid=(steps,),
        out_shape=out_shape,
        in_specs=[
            rows_spec,
            rows_spec,
            pl.BlockSpec(work.shape, lambda i: (0, 0)),
            pl.BlockSpec((step, 1), lambda i: (i, 0)),
        ]
        + [rows_spec] * last,
        out_specs=out_specs,
        compiler_params=pltpu.CompilerParams(vmem_limit_bytes=56 * 1024 * 1024),
        name="expert_front",
    )(normed_all, cotangent_all, work, weight, *([before] * last))


def expert_grads(normed_all, pair_grad, cotangent_all, hidden):
    seq, width = normed_all.shape
    step = 256

    def body(rows_ref, pair_ref, back_ref, hidden_ref, out_ref):
        contract = (((0,), (0,)), ((), ()))
        out_ref[:, : 2 * FF] = lax.dot_general(
            rows_ref[...], pair_ref[...], contract, preferred_element_type=jnp.float32
        ).astype(jnp.bfloat16)
        out_ref[:, 2 * FF :] = lax.dot_general(
            back_ref[...], hidden_ref[...], contract, preferred_element_type=jnp.float32
        ).astype(jnp.bfloat16)

    cols_spec = pl.BlockSpec((seq, step), lambda i: (0, i))
    return pl.pallas_call(
        body,
        grid=(width // step,),
        out_shape=jax.ShapeDtypeStruct((width, 3 * FF), jnp.bfloat16),
        in_specs=[
            cols_spec,
            pl.BlockSpec(pair_grad.shape, lambda i: (0, 0)),
            cols_spec,
            pl.BlockSpec(hidden.shape, lambda i: (0, 0)),
        ],
        out_specs=pl.BlockSpec((step, 3 * FF), lambda i: (i, 0)),
        compiler_params=pltpu.CompilerParams(vmem_limit_bytes=56 * 1024 * 1024),
        name="expert_grads",
    )(normed_all, pair_grad, cotangent_all, hidden)


def expert_value(hidden, works):
    seq = hidden[0].shape[0]
    n_exp = len(works)
    width = works[0].shape[0]
    step = EXPERT_STEP
    half = seq // step // 2

    def body(*refs):
        even_ref, odd_ref = refs[2 * n_exp :]
        total = jnp.zeros((step, width), jnp.float32)
        for e in range(n_exp):
            total = total + lax.dot_general(
                refs[e][...],
                refs[n_exp + e][...],
                (((1,), (1,)), ((), ())),
                preferred_element_type=jnp.float32,
            )

        @pl.when(pl.program_id(0) < half)
        def _():
            even_ref[...] = total

        @pl.when(pl.program_id(0) >= half)
        def _():
            odd_ref[...] = total.astype(jnp.bfloat16)

    return pl.pallas_call(
        body,
        grid=(seq // step,),
        out_shape=[
            jax.ShapeDtypeStruct((seq // 2, width), jnp.float32),
            jax.ShapeDtypeStruct((seq // 2, width), jnp.bfloat16),
        ],
        in_specs=[pl.BlockSpec((step, FF), lambda i: (i, 0))] * n_exp
        + [pl.BlockSpec((width, FF), lambda i: (0, 2))] * n_exp,
        out_specs=[
            pl.BlockSpec((step, width), lambda i: (jnp.minimum(i, half - 1), 0)),
            pl.BlockSpec((step, width), lambda i: (jnp.maximum(i - half, 0), 0)),
        ],
        compiler_params=pltpu.CompilerParams(vmem_limit_bytes=56 * 1024 * 1024),
        name="expert_value",
    )(*hidden, *works)


def local(
    hidden_in,
    out_cotangent,
    routes,
    route_probs,
    norm_gains,
    qkv_weight,
    out_weight,
    expert_up,
    expert_down,
    norm_gains_first,
    qkv_weight_first,
    out_weight_first,
    expert_up_first,
    expert_down_first,
    norm_gains_second,
    qkv_weight_second,
    out_weight_second,
    expert_up_second,
    expert_down_second,
):
    f32 = jnp.float32
    bf16 = jnp.bfloat16
    both = ("ctx", "fsdp")
    n_ctx = lax.axis_size("ctx")
    n_fsdp = lax.axis_size("fsdp")
    n_all = n_ctx * n_fsdp
    ctx_index = lax.axis_index("ctx")
    n_exp = expert_up.shape[0]
    shard = qkv_weight.shape[0]
    seq = DEVICE_TOKENS * n_ctx
    q_dev = QUERY_HEADS // n_ctx
    kv_dev = max(1, KEY_VALUE_HEADS // n_ctx)
    share = max(1, n_ctx // KEY_VALUE_HEADS)
    q_cols = q_dev * HEAD_SIZE
    kv_cols = kv_dev * HEAD_SIZE
    cols = q_cols + 2 * kv_cols

    tokens = hidden_in[0]
    cotangent = out_cotangent[0]

    expert_shards = [
        jnp.concatenate([expert_up[e].astype(bf16), expert_down[e].astype(bf16).T], 1)
        for e in range(n_exp)
    ]
    expert_shards[0], tokens = lax.optimization_barrier((expert_shards[0], tokens))
    expert_works = [lax.all_gather(part, "fsdp", axis=0, tiled=True) for part in expert_shards]
    inv_first = lax.rsqrt(jnp.mean(tokens * tokens, -1, keepdims=True) + NORM_EPS)
    unit_rows = (tokens * inv_first).astype(bf16)
    unit_all = gather_rows(unit_rows)

    gain_shard = norm_gains.astype(bf16).astype(f32)
    qkv_shard = qkv_weight.astype(bf16).astype(f32)
    scaled = (qkv_shard * gain_shard[0][:, None]).astype(bf16)
    q_part = scaled[:, :QUERY_FEATURES].reshape(shard, n_ctx, q_cols)
    k_part = scaled[:, QUERY_FEATURES : QUERY_FEATURES + KEY_FEATURES]
    v_part = scaled[:, QUERY_FEATURES + KEY_FEATURES :]
    k_part = jnp.repeat(k_part.reshape(shard, n_ctx // share, kv_cols), share, 1)
    v_part = jnp.repeat(v_part.reshape(shard, n_ctx // share, kv_cols), share, 1)
    head_cols = jnp.concatenate([q_part, k_part, v_part], -1).transpose(1, 0, 2)
    head_group = lax.all_to_all(head_cols, "ctx", split_axis=0, concat_axis=0, tiled=True)
    head_group = head_group.reshape(n_ctx * shard, cols)
    qkv_heads = assemble_heads(
        [head_group] + [exchange(head_group, "fsdp", mask) for mask in range(1, n_fsdp)], shard
    )

    gain_row = jnp.pad(norm_gains[1:2].astype(bf16), ((0, 7), (0, MODEL_WIDTH - shard)))
    out_shard = jnp.concatenate([out_weight.astype(bf16), gain_row], 0)
    out_group = [out_shard] + [exchange(out_shard, "fsdp", mask) for mask in range(1, n_fsdp)]

    experts = jnp.arange(n_exp * n_ctx, dtype=jnp.int32)
    chosen = routes[0][:, None, :] == experts[None, :, None]
    weight_rows = jnp.sum(jnp.where(chosen, route_probs[0][:, None, :], 0.0), 2).T
    weight_high = lax.reduce_precision(weight_rows, 8, 7)
    weight_low = weight_rows - weight_high
    weight_flat = jnp.stack([weight_high, weight_low]).reshape(-1, MODEL_WIDTH).astype(bf16)
    gain_flat = jnp.concatenate([part[shard : shard + 1, :shard] for part in out_group], 1)
    gain_flat = jnp.pad(gain_flat, ((0, 0), (0, MODEL_WIDTH - n_fsdp * shard)))
    n_misc = weight_flat.shape[0]
    misc_rows = -(-(n_misc + 1) // 16) * 16
    payload = jnp.concatenate(
        [
            (RES_SCALE * cotangent).astype(bf16),
            *[part[:shard] for part in out_group],
            weight_flat,
            gain_flat,
            jnp.zeros((misc_rows - n_misc - 1, MODEL_WIDTH), bf16),
        ],
        0,
    )

    def out_place(mask_fsdp):
        def place(k, mask, ctx, fsdp):
            return ((ctx ^ mask) * n_fsdp + (fsdp ^ mask_fsdp)) * shard

        return place

    payload_pieces = row_pieces(payload)

    moves = [(0, DEVICE_TOKENS, 0, lambda k, mask, ctx, fsdp: k * DEVICE_TOKENS)]
    for mask_fsdp in range(n_fsdp):
        moves.append((DEVICE_TOKENS + mask_fsdp * shard, shard, 1, out_place(mask_fsdp)))
    moves.append(
        (DEVICE_TOKENS + q_cols, misc_rows, 2, lambda k, mask, ctx, fsdp: k * misc_rows)
    )
    device_ids = ctx_index ^ jnp.array(relative_order(n_ctx), jnp.int32)
    row_ids = device_ids[:, None] * DEVICE_TOKENS + jnp.arange(DEVICE_TOKENS, dtype=jnp.int32)
    position = positions(row_ids.reshape(-1), DEVICE_TOKENS, n_ctx)
    cosine_table, sine_table = rope_tables(position, HEAD_SIZE)

    projected = jnp.dot(unit_all, qkv_heads, preferred_element_type=f32)
    query_heads = (
        apply_rotary(
            projected[:, :q_cols].reshape(seq, q_dev, HEAD_SIZE), cosine_table, sine_table
        )
        .astype(bf16)
        .reshape(seq, kv_dev, q_dev // kv_dev, HEAD_SIZE)
    )
    key_heads = apply_rotary(
        projected[:, q_cols : q_cols + kv_cols].reshape(seq, kv_dev, HEAD_SIZE),
        cosine_table,
        sine_table,
    ).astype(bf16)
    value_heads = projected[:, q_cols + kv_cols :].astype(bf16).reshape(seq, kv_dev, HEAD_SIZE)
    attended, logarithm_total = attend(query_heads, key_heads, value_heads, position, position)
    attended_rows = attended.reshape(seq, q_cols)
    attended_natural = reorder(attended_rows, n_ctx, True)
    attended_natural, payload_pieces = lax.optimization_barrier(
        (attended_natural, payload_pieces)
    )
    attn_rows = lax.all_to_all(attended_natural, "ctx", 0, 0, tiled=True)
    cotangent_all, out_all, misc_all = assemble(
        payload_pieces, [seq, MODEL_WIDTH, n_ctx * misc_rows], moves
    )
    misc_all = misc_all.reshape(n_ctx, misc_rows, MODEL_WIDTH)
    weight_all = (
        misc_all[:, :n_misc]
        .astype(f32)
        .reshape(n_ctx, 2, n_exp * n_ctx, DEVICE_TOKENS)
    )
    weight_all = lax.dynamic_slice_in_dim(
        weight_all[:, 0] + weight_all[:, 1], ctx_index * n_exp, n_exp, 1
    )
    weight_own = weight_all.transpose(0, 2, 1).reshape(seq, n_exp)
    gain_pieces = misc_all[:, n_misc, : n_fsdp * shard].astype(f32)
    group_ids = lax.axis_index("fsdp") ^ jnp.arange(n_fsdp, dtype=jnp.int32)
    piece_ids = (device_ids[:, None] * n_fsdp + group_ids[None, :]).reshape(n_all)
    is_piece = piece_ids[None, :] == jnp.arange(n_all, dtype=jnp.int32)[:, None]
    gain_ffn = jnp.sum(
        jnp.where(is_piece[:, :, None], gain_pieces.reshape(1, n_all, shard), 0.0), 1
    ).reshape(1, MODEL_WIDTH)

    residual, normed_ffn = project_out(attn_rows, out_all, tokens, gain_ffn)

    normed_all = gather_rows(normed_ffn)
    hidden = []
    expert_rows = []
    sums = [None]
    half = seq // 2
    for e in range(n_exp):
        weighted_hidden, pair_grad, *sums = expert_front(
            normed_all, cotangent_all, expert_works[e], weight_own[:, e : e + 1], sums[0]
        )
        if e == n_exp - 1:
            own_grad, grad_parts = pair_parts(*sums)
            grad_parts, weighted_hidden, pair_grad = lax.optimization_barrier(
                (grad_parts, weighted_hidden, pair_grad)
            )
            other_grads = send_parts(grad_parts)
        hidden.append(weighted_hidden)
        expert_term = expert_grads(normed_all, pair_grad, cotangent_all, weighted_hidden)
        if e < n_exp - 1:
            expert_works[e + 1], expert_term = lax.optimization_barrier(
                (expert_works[e + 1], expert_term)
            )
        expert_part = lax.psum_scatter(expert_term, "fsdp", scatter_dimension=0, tiled=True)
        expert_rows.append(with_layout_constraint(expert_part, Layout(major_to_minor=(0, 1))))
    value_sums = expert_value(hidden, expert_works)
    own_grad, value_sums = lax.optimization_barrier((own_grad, value_sums))

    residual_grad, attn_grad, gain_ffn_part, head_grads = residual_back(
        own_grad, other_grads, residual, cotangent, gain_ffn, out_all
    )
    gain_ffn_part = gain_ffn_part[0]
    hidden_out = residual + RES_SCALE * scatter_sum(*value_sums)
    attn_out_heads = reorder(
        lax.all_to_all(head_grads, "ctx", 0, 0, tiled=True), n_ctx, False
    )
    query_gradient, key_gradient, value_gradient = attend_back(
        query_heads,
        key_heads,
        value_heads,
        attended,
        attn_out_heads.reshape(seq, kv_dev, q_dev // kv_dev, HEAD_SIZE),
        logarithm_total,
        position,
        position,
    )
    query_rows = inverse_rotary(
        query_gradient.reshape(seq, q_dev, HEAD_SIZE), cosine_table, sine_table
    )
    key_rows = inverse_rotary(key_gradient, cosine_table, sine_table)
    qkv_rows = jnp.concatenate(
        [
            query_rows.reshape(seq, q_cols),
            key_rows.reshape(seq, kv_cols),
            value_gradient.reshape(seq, kv_cols),
        ],
        1,
    ).astype(bf16)
    grad_all = gather_rows(attn_grad)
    out_term = lax.dot_general(
        attended_rows, grad_all, (((0,), (0,)), ((), ())), preferred_element_type=f32
    ).astype(bf16)
    out_term, qkv_rows = lax.optimization_barrier((out_term, qkv_rows))

    def in_grad_rows(rows):
        return lax.dot_general(
            rows, qkv_heads, (((1,), (1,)), ((), ())), preferred_element_type=f32
        )

    odd_in_grad = in_grad_rows(qkv_rows[half:]).astype(bf16)
    scaled_in_grad, in_parts = pair_parts(in_grad_rows(qkv_rows[:half]), odd_in_grad)
    in_parts, qkv_rows = lax.optimization_barrier((in_parts, qkv_rows))
    for part in send_parts(in_parts):
        scaled_in_grad = scaled_in_grad + part.astype(f32)
    up_grad_shard = jnp.stack([part[:, : 2 * FF] for part in expert_rows]).astype(f32)
    down_grad_shard = with_layout_constraint(
        jnp.stack([part[:, 2 * FF :].astype(f32).T for part in expert_rows]),
        Layout(major_to_minor=(0, 1, 2)),
    )
    input_grad = (
        residual_grad
        + inv_first * scaled_in_grad
        - tokens * inv_first**3 * jnp.mean(scaled_in_grad * tokens, -1, keepdims=True)
    )

    fsdp_index = lax.axis_index("fsdp")

    def out_block(mask):
        return lax.dynamic_slice_in_dim(out_term, (fsdp_index ^ mask) * shard, shard, 0)

    out_grad = out_block(0).astype(f32)
    for mask in range(1, n_fsdp):
        out_grad = out_grad + exchange(out_block(mask), "fsdp", mask).astype(f32)
    qkv_term = lax.dot_general(
        unit_all, qkv_rows, (((0,), (0,)), ((), ())), preferred_element_type=f32
    ).astype(bf16)
    gain_high = lax.reduce_precision(gain_ffn_part, 8, 7)
    gain_parts = jnp.stack([gain_high, gain_ffn_part - gain_high]).reshape(2, n_all, shard)
    gain_parts = jnp.pad(
        gain_parts.transpose(1, 0, 2).astype(bf16), ((0, 0), (0, 6), (0, cols - shard))
    )
    qkv_pieces = lax.all_to_all(
        jnp.concatenate([qkv_term.reshape(n_all, shard, cols), gain_parts], 1),
        both,
        0,
        0,
        tiled=True,
    ).reshape(n_ctx, n_fsdp, shard + 8, cols)
    gain_ffn_grad = jnp.sum(qkv_pieces[:, :, shard : shard + 2, :shard].astype(f32), (0, 1, 2))
    qkv_pieces = qkv_pieces[:, :, :shard]
    qkv_sum = jnp.sum(qkv_pieces.astype(f32), 1)
    kv_sum = jnp.sum(
        qkv_sum[..., q_cols:].reshape(n_ctx // share, share, shard, 2, kv_cols), 1
    ).transpose(1, 2, 0, 3)
    unit_grad = jnp.concatenate(
        [
            qkv_sum[..., :q_cols].transpose(1, 0, 2).reshape(shard, QUERY_FEATURES),
            kv_sum.reshape(shard, 2 * KEY_FEATURES),
        ],
        1,
    )
    qkv_grad = gain_shard[0][:, None] * unit_grad
    gain_attn_grad = jnp.sum(qkv_shard * unit_grad, 1)
    gains_grad = jnp.stack([gain_attn_grad, gain_ffn_grad])

    norm_new = adamw_update(norm_gains, gains_grad, norm_gains_first, norm_gains_second, 0.0)
    qkv_new = adamw_update(qkv_weight, qkv_grad, qkv_weight_first, qkv_weight_second, WEIGHT_DECAY)
    out_new = adamw_update(out_weight, out_grad, out_weight_first, out_weight_second, WEIGHT_DECAY)
    up_new = adamw_update(expert_up, up_grad_shard, expert_up_first, expert_up_second, WEIGHT_DECAY)
    down_new = adamw_update(
        expert_down, down_grad_shard, expert_down_first, expert_down_second, WEIGHT_DECAY
    )
    return (
        hidden_out[None],
        input_grad[None],
        gains_grad,
        qkv_grad,
        out_grad,
        up_grad_shard,
        down_grad_shard,
        norm_new[0],
        qkv_new[0],
        out_new[0],
        up_new[0],
        down_new[0],
        norm_new[1],
        qkv_new[1],
        out_new[1],
        up_new[1],
        down_new[1],
        norm_new[2],
        qkv_new[2],
        out_new[2],
        up_new[2],
        down_new[2],
    )


def solution(mesh):
    in_specs = (
        P("fsdp", "ctx", None),
        P("fsdp", "ctx", None),
        P("fsdp", "ctx", None),
        P("fsdp", "ctx", None),
        P(None, ("ctx", "fsdp")),
        P(("ctx", "fsdp"), None),
        P(("ctx", "fsdp"), None),
        P("ctx", "fsdp", None),
        P("ctx", None, "fsdp"),
        P(None, ("ctx", "fsdp")),
        P(("ctx", "fsdp"), None),
        P(("ctx", "fsdp"), None),
        P("ctx", "fsdp", None),
        P("ctx", None, "fsdp"),
        P(None, ("ctx", "fsdp")),
        P(("ctx", "fsdp"), None),
        P(("ctx", "fsdp"), None),
        P("ctx", "fsdp", None),
        P("ctx", None, "fsdp"),
    )
    out_specs = (
        P("fsdp", "ctx", None),
        P("fsdp", "ctx", None),
        P(None, ("ctx", "fsdp")),
        P(("ctx", "fsdp"), None),
        P(("ctx", "fsdp"), None),
        P("ctx", "fsdp", None),
        P("ctx", None, "fsdp"),
        P(None, ("ctx", "fsdp")),
        P(("ctx", "fsdp"), None),
        P(("ctx", "fsdp"), None),
        P("ctx", "fsdp", None),
        P("ctx", None, "fsdp"),
        P(None, ("ctx", "fsdp")),
        P(("ctx", "fsdp"), None),
        P(("ctx", "fsdp"), None),
        P("ctx", "fsdp", None),
        P("ctx", None, "fsdp"),
        P(None, ("ctx", "fsdp")),
        P(("ctx", "fsdp"), None),
        P(("ctx", "fsdp"), None),
        P("ctx", "fsdp", None),
        P("ctx", None, "fsdp"),
    )
    return jax.shard_map(local, mesh=mesh, in_specs=in_specs, out_specs=out_specs, check_vma=False)
```

```python
import jax
import jax.numpy as jnp
from jax import lax
from jax.experimental import pallas as pl
from jax.experimental.layout import Layout, with_layout_constraint
from jax.experimental.pallas import tpu as pltpu
from jax.sharding import PartitionSpec as P

MODEL_WIDTH = 1024
QUERY_HEADS = 16
KEY_VALUE_HEADS = 8
HEAD_SIZE = 64
FF = 512
TOP = 8
DEVICE_TOKENS = 128
QUERY_FEATURES = 1024
KEY_FEATURES = 512


RES_SCALE = 0.22
SCORE_SCALE = 0.015625
NORM_EPS = 1e-06
ROPE_BASE = 10000.0
LEARN_RATE = 0.02
BETA_FIRST = 0.9
BETA_SECOND = 0.999
ADAM_EPS = 1e-08
WEIGHT_DECAY = 0.1
ADAM_STEP = 3.0
MASK_VALUE = -1e30
EXPERT_STEP = 256


def positions(row_ids, tok_dev, n_ctx):
    device = row_ids // tok_dev
    within = row_ids % tok_dev
    half_block = tok_dev // 2
    return jnp.where(
        within < half_block,
        device * half_block + within,
        (2 * n_ctx - 1 - device) * half_block + within - half_block,
    )


def rope_tables(position, head_dim):
    half_dim = head_dim // 2
    frequency = ROPE_BASE ** (-(jnp.arange(half_dim, dtype=jnp.float32) * 2.0 / head_dim))
    angles = position.astype(jnp.float32)[:, None] * frequency[None, :]
    return (jnp.cos(angles)[:, None, :], jnp.sin(angles)[:, None, :])


def apply_rotary(values, cosine_table, sine_table):
    half_dim = values.shape[-1] // 2
    lower_half, upper_half = (values[..., :half_dim], values[..., half_dim:])
    return jnp.concatenate(
        [
            lower_half * cosine_table - upper_half * sine_table,
            upper_half * cosine_table + lower_half * sine_table,
        ],
        -1,
    )


def inverse_rotary(cotangent, cosine_table, sine_table):
    half_dim = cotangent.shape[-1] // 2
    lower_half, upper_half = (cotangent[..., :half_dim], cotangent[..., half_dim:])
    return jnp.concatenate(
        [
            lower_half * cosine_table + upper_half * sine_table,
            upper_half * cosine_table - lower_half * sine_table,
        ],
        -1,
    )


def scores_of(queries, key_head_rows, q_pos, k_pos):
    raw_scores = jnp.einsum(
        "qgrd,kgd->grqk", queries, key_head_rows, preferred_element_type=jnp.float32
    )
    raw_scores = raw_scores * SCORE_SCALE
    allowed = k_pos[None, :] <= q_pos[:, None]
    return jnp.where(allowed, raw_scores, MASK_VALUE)


def attend(queries, key_head_rows, value_head_rows, q_pos, k_pos):
    scores = scores_of(queries, key_head_rows, q_pos, k_pos)
    row_max = jnp.max(scores, -1, keepdims=True)
    logarithm_total = row_max + jnp.log(jnp.sum(jnp.exp(scores - row_max), -1, keepdims=True))
    attn_probs = jnp.exp(scores - logarithm_total).astype(jnp.bfloat16)
    output = jnp.einsum(
        "grqk,kgd->qgrd", attn_probs, value_head_rows, preferred_element_type=jnp.float32
    ).astype(jnp.bfloat16)
    return (output, logarithm_total)


def attend_back(
    queries, key_head_rows, value_head_rows, output, out_grad, logarithm_total, q_pos, k_pos
):
    scores = scores_of(queries, key_head_rows, q_pos, k_pos)
    attn_probs = jnp.exp(scores - logarithm_total)
    value_gradient = jnp.einsum(
        "grqk,qgrd->kgd",
        attn_probs.astype(jnp.bfloat16),
        out_grad,
        preferred_element_type=jnp.float32,
    )
    prob_grad = jnp.einsum(
        "qgrd,kgd->grqk", out_grad, value_head_rows, preferred_element_type=jnp.float32
    )
    row_dot = jnp.einsum("qgrd,qgrd->grq", out_grad, output, preferred_element_type=jnp.float32)[
        ..., None
    ]
    score_grad = (attn_probs * (prob_grad - row_dot) * SCORE_SCALE).astype(jnp.bfloat16)
    query_gradient = jnp.einsum(
        "grqk,kgd->qgrd", score_grad, key_head_rows, preferred_element_type=jnp.float32
    )
    key_gradient = jnp.einsum(
        "grqk,qgrd->kgd", score_grad, queries, preferred_element_type=jnp.float32
    )
    return (query_gradient, key_gradient, value_gradient)


def adamw_update(weight, gradient, first_moment, second_moment, decay_rate):
    first_new = BETA_FIRST * first_moment + (1.0 - BETA_FIRST) * gradient
    second_new = BETA_SECOND * second_moment + (1.0 - BETA_SECOND) * gradient * gradient
    first_hat = first_new / (1.0 - BETA_FIRST**ADAM_STEP)
    second_hat = second_new / (1.0 - BETA_SECOND**ADAM_STEP)
    weight_new = weight - LEARN_RATE * (
        first_hat / (jnp.sqrt(second_hat) + ADAM_EPS) + decay_rate * weight
    )
    return (weight_new, first_new, second_new)


def xor_perm(size, mask):
    return [(i, i ^ mask) for i in range(size)]


def exchange(values, axis, mask):
    return lax.ppermute(values, axis, xor_perm(lax.axis_size(axis), mask))


def relative_order(size):
    return list(range(0, size, 2)) + list(range(1, size, 2))


def assemble(pieces, sizes, moves):
    count = len(pieces)
    order = relative_order(count)

    def body(index_ref, *refs):
        outs = refs[count : count + len(sizes)]
        copies = []
        for k in range(count):
            for m, (start, length, number, place) in enumerate(moves):
                at = place(k, order[k], index_ref[0], index_ref[1])
                if not isinstance(at, int):
                    at = pl.multiple_of(at, length)
                copies.append(
                    pltpu.make_async_copy(
                        refs[k].at[pl.ds(start, length)],
                        outs[number].at[pl.ds(at, length)],
                        refs[-1].at[k, m],
                    )
                )
        for copy in copies:
            copy.start()
        for copy in copies:
            copy.wait()

    width = pieces[0].shape[1]
    return pl.pallas_call(
        body,
        out_shape=[jax.ShapeDtypeStruct((size, width), pieces[0].dtype) for size in sizes],
        in_specs=[pl.BlockSpec(memory_space=pltpu.SMEM)]
        + [pl.BlockSpec(memory_space=pl.ANY)] * count,
        out_specs=[pl.BlockSpec(memory_space=pltpu.VMEM)] * len(sizes),
        scratch_shapes=[pltpu.SemaphoreType.DMA((count, len(moves)))],
        name="assemble",
    )(jnp.concatenate([device_index("ctx"), device_index("fsdp")]), *pieces)


def assemble_heads(pieces, shard):
    size = len(pieces)
    rows, cols = pieces[0].shape
    count = rows // shard

    def body(index_ref, *refs):
        copies = []
        for mask in range(size):
            for i in range(count):
                at = pl.multiple_of((i * size + (index_ref[0] ^ mask)) * shard, shard)
                copies.append(
                    pltpu.make_async_copy(
                        refs[mask].at[pl.ds(i * shard, shard)],
                        refs[size].at[pl.ds(at, shard)],
                        refs[-1].at[mask, i],
                    )
                )
        for copy in copies:
            copy.start()
        for copy in copies:
            copy.wait()

    return pl.pallas_call(
        body,
        out_shape=jax.ShapeDtypeStruct((rows * size, cols), pieces[0].dtype),
        in_specs=[pl.BlockSpec(memory_space=pltpu.SMEM)]
        + [pl.BlockSpec(memory_space=pl.ANY)] * size,
        out_specs=pl.BlockSpec(memory_space=pltpu.VMEM),
        scratch_shapes=[pltpu.SemaphoreType.DMA((size, count))],
        name="assemble_heads",
    )(device_index("fsdp"), *pieces)


def device_index(axis):
    return lax.axis_index(axis).astype(jnp.int32).reshape(1)


def reorder(rows, count, to_natural):
    length = rows.shape[0] // count
    order = relative_order(count)

    def body(index_ref, rows_ref, out_ref):
        for place in range(count):
            there = pl.ds(pl.multiple_of((index_ref[0] ^ order[place]) * length, length), length)
            here = pl.ds(place * length, length)
            if to_natural:
                out_ref[there, :] = rows_ref[here, :]
            else:
                out_ref[here, :] = rows_ref[there, :]

    return pl.pallas_call(
        body,
        out_shape=jax.ShapeDtypeStruct(rows.shape, rows.dtype),
        in_specs=[
            pl.BlockSpec(memory_space=pltpu.SMEM),
            pl.BlockSpec(memory_space=pltpu.VMEM),
        ],
        out_specs=pl.BlockSpec(memory_space=pltpu.VMEM),
        name="reorder",
    )(device_index("ctx"), rows)


def project_out(heads, out_all, tokens, gain):
    count = heads.shape[0] // tokens.shape[0]
    length, width = tokens.shape
    cols = heads.shape[1]

    def body(heads_ref, out_ref, tokens_ref, gain_ref, residual_ref, normed_ref):
        total = jnp.zeros((length, width), jnp.float32)
        for place in range(count):
            total = total + jnp.dot(
                heads_ref[place * length : (place + 1) * length, :],
                out_ref[place * cols : (place + 1) * cols, :],
                preferred_element_type=jnp.float32,
            )
        residual = tokens_ref[...] + RES_SCALE * total
        inv = lax.rsqrt(jnp.mean(residual * residual, -1, keepdims=True) + NORM_EPS)
        residual_ref[...] = residual
        normed_ref[...] = (residual * inv * gain_ref[...]).astype(jnp.bfloat16)

    vmem = pl.BlockSpec(memory_space=pltpu.VMEM)
    return pl.pallas_call(
        body,
        out_shape=[
            jax.ShapeDtypeStruct((length, width), jnp.float32),
            jax.ShapeDtypeStruct((length, width), jnp.bfloat16),
        ],
        in_specs=[vmem] * 4,
        out_specs=[vmem] * 2,
        name="project_out",
    )(heads, out_all, tokens, gain)


def residual_back(own, received, residual, cotangent, gain, out_all):
    length, width = residual.shape
    count = lax.axis_size("ctx")
    cols = out_all.shape[0] // count
    n_parts = len(received)

    def body(own_ref, *refs):
        parts = refs[:n_parts]
        residual_ref, cotangent_ref, gain_ref, out_ref = refs[n_parts : n_parts + 4]
        grad_ref, attn_ref, gain_grad_ref, heads_ref = refs[n_parts + 4 :]
        ffn_grad = own_ref[...]
        for part in parts:
            ffn_grad = ffn_grad + part[...].astype(jnp.float32)
        rows = residual_ref[...]
        inv = lax.rsqrt(jnp.mean(rows * rows, -1, keepdims=True) + NORM_EPS)
        weighted = gain_ref[...] * ffn_grad
        gain_grad_ref[...] = jnp.sum(ffn_grad * rows * inv, 0, keepdims=True)
        grad = (
            cotangent_ref[...]
            + inv * weighted
            - rows * (inv * inv * inv) * jnp.mean(weighted * rows, -1, keepdims=True)
        )
        grad_ref[...] = grad
        attn_grad = (RES_SCALE * grad).astype(jnp.bfloat16)
        attn_ref[...] = attn_grad
        for place in range(count):
            heads_ref[place * length : (place + 1) * length, :] = lax.dot_general(
                attn_grad,
                out_ref[place * cols : (place + 1) * cols, :],
                (((1,), (1,)), ((), ())),
                preferred_element_type=jnp.float32,
            ).astype(jnp.bfloat16)

    vmem = pl.BlockSpec(memory_space=pltpu.VMEM)
    return pl.pallas_call(
        body,
        out_shape=[
            jax.ShapeDtypeStruct((length, width), jnp.float32),
            jax.ShapeDtypeStruct((length, width), jnp.bfloat16),
            jax.ShapeDtypeStruct((1, width), jnp.float32),
            jax.ShapeDtypeStruct((count * length, cols), jnp.bfloat16),
        ],
        in_specs=[vmem] * (5 + n_parts),
        out_specs=[vmem] * 4,
        name="residual_back",
    )(own, *received, residual, cotangent, gain, out_all)


def row_pieces(rows):
    size = lax.axis_size("ctx")
    even = [rows] + [exchange(rows, "ctx", mask) for mask in range(2, size, 2)]
    return even + [exchange(piece, "ctx", 1) for piece in even]


def gather_rows(rows):
    length = rows.shape[0]
    pieces = row_pieces(rows)
    move = (0, length, 0, lambda k, mask, ctx, fsdp: k * length)
    return assemble(pieces, [length * len(pieces)], [move])[0]


def pair_parts(even_rows, odd_rows):
    size = lax.axis_size("ctx")
    block = even_rows.shape[0] * 2 // size
    pair_sum = even_rows + exchange(odd_rows, "ctx", 1).astype(jnp.float32)
    parts = [
        pair_sum[place * block : (place + 1) * block].astype(jnp.bfloat16)
        for place in range(1, size // 2)
    ]
    return pair_sum[:block], parts


def send_parts(parts):
    return [exchange(part, "ctx", 2 * place + 2) for place, part in enumerate(parts)]


def scatter_sum(even_rows, odd_rows):
    total, parts = pair_parts(even_rows, odd_rows)
    for part in send_parts(parts):
        total = total + part.astype(jnp.float32)
    return total


def expert_front(normed_all, cotangent_all, work, weight, before):
    seq, width = normed_all.shape
    step = EXPERT_STEP
    steps = seq // step
    half = steps // 2
    last = before is not None

    def body(rows_ref, back_ref, work_ref, weight_ref, *refs):
        if last:
            before_ref, hidden_ref, pair_ref, even_ref, odd_ref = refs
        else:
            hidden_ref, pair_ref, even_ref = refs
        gate_up = jnp.dot(rows_ref[...], work_ref[:, : 2 * FF], preferred_element_type=jnp.float32)
        gate = gate_up[:, :FF]
        up = gate_up[:, FF:]
        sig = 1.0 / (1.0 + jnp.exp(-gate))
        act = gate * sig
        hidden_ref[...] = (weight_ref[...] * (act * up)).astype(jnp.bfloat16)
        back = weight_ref[...] * jnp.dot(
            back_ref[...], work_ref[:, 2 * FF :], preferred_element_type=jnp.float32
        )
        pair_ref[:, :FF] = (back * up * sig * (1.0 + gate * (1.0 - sig))).astype(jnp.bfloat16)
        pair_ref[:, FF:] = (back * act).astype(jnp.bfloat16)
        total = lax.dot_general(
            pair_ref[...],
            work_ref[:, : 2 * FF],
            (((1,), (1,)), ((), ())),
            preferred_element_type=jnp.float32,
        )
        if not last:
            even_ref[...] = total
        else:
            total = total + before_ref[...]

            @pl.when(pl.program_id(0) < half)
            def _():
                even_ref[...] = total

            @pl.when(pl.program_id(0) >= half)
            def _():
                odd_ref[...] = total.astype(jnp.bfloat16)

    rows_spec = pl.BlockSpec((step, width), lambda i: (i, 0))
    out_shape = [
        jax.ShapeDtypeStruct((seq, FF), jnp.bfloat16),
        jax.ShapeDtypeStruct((seq, 2 * FF), jnp.bfloat16),
    ]
    out_specs = [
        pl.BlockSpec((step, FF), lambda i: (i, 0)),
        pl.BlockSpec((step, 2 * FF), lambda i: (i, 0)),
    ]
    if last:
        out_shape += [
            jax.ShapeDtypeStruct((seq // 2, width), jnp.float32),
            jax.ShapeDtypeStruct((seq // 2, width), jnp.bfloat16),
        ]
        out_specs += [
            pl.BlockSpec((step, width), lambda i: (jnp.minimum(i, half - 1), 0)),
            pl.BlockSpec((step, width), lambda i: (jnp.maximum(i - half, 0), 0)),
        ]
    else:
        out_shape.append(jax.ShapeDtypeStruct((seq, width), jnp.float32))
        out_specs.append(rows_spec)
    return pl.pallas_call(
        body,
        grid=(steps,),
        out_shape=out_shape,
        in_specs=[
            rows_spec,
            rows_spec,
            pl.BlockSpec(work.shape, lambda i: (0, 0)),
            pl.BlockSpec((step, 1), lambda i: (i, 0)),
        ]
        + [rows_spec] * last,
        out_specs=out_specs,
        compiler_params=pltpu.CompilerParams(vmem_limit_bytes=56 * 1024 * 1024),
        name="expert_front",
    )(normed_all, cotangent_all, work, weight, *([before] * last))


def expert_grads(normed_all, pair_grad, cotangent_all, hidden):
    seq, width = normed_all.shape
    step = 256

    def body(rows_ref, pair_ref, back_ref, hidden_ref, out_ref):
        contract = (((0,), (0,)), ((), ()))
        out_ref[:, : 2 * FF] = lax.dot_general(
            rows_ref[...], pair_ref[...], contract, preferred_element_type=jnp.float32
        ).astype(jnp.bfloat16)
        out_ref[:, 2 * FF :] = lax.dot_general(
            back_ref[...], hidden_ref[...], contract, preferred_element_type=jnp.float32
        ).astype(jnp.bfloat16)

    cols_spec = pl.BlockSpec((seq, step), lambda i: (0, i))
    return pl.pallas_call(
        body,
        grid=(width // step,),
        out_shape=jax.ShapeDtypeStruct((width, 3 * FF), jnp.bfloat16),
        in_specs=[
            cols_spec,
            pl.BlockSpec(pair_grad.shape, lambda i: (0, 0)),
            cols_spec,
            pl.BlockSpec(hidden.shape, lambda i: (0, 0)),
        ],
        out_specs=pl.BlockSpec((step, 3 * FF), lambda i: (i, 0)),
        compiler_params=pltpu.CompilerParams(vmem_limit_bytes=56 * 1024 * 1024),
        name="expert_grads",
    )(normed_all, pair_grad, cotangent_all, hidden)


def expert_value(hidden, works):
    seq = hidden[0].shape[0]
    n_exp = len(works)
    width = works[0].shape[0]
    step = EXPERT_STEP
    half = seq // step // 2

    def body(*refs):
        even_ref, odd_ref = refs[2 * n_exp :]
        total = jnp.zeros((step, width), jnp.float32)
        for e in range(n_exp):
            total = total + lax.dot_general(
                refs[e][...],
                refs[n_exp + e][...],
                (((1,), (1,)), ((), ())),
                preferred_element_type=jnp.float32,
            )

        @pl.when(pl.program_id(0) < half)
        def _():
            even_ref[...] = total

        @pl.when(pl.program_id(0) >= half)
        def _():
            odd_ref[...] = total.astype(jnp.bfloat16)

    return pl.pallas_call(
        body,
        grid=(seq // step,),
        out_shape=[
            jax.ShapeDtypeStruct((seq // 2, width), jnp.float32),
            jax.ShapeDtypeStruct((seq // 2, width), jnp.bfloat16),
        ],
        in_specs=[pl.BlockSpec((step, FF), lambda i: (i, 0))] * n_exp
        + [pl.BlockSpec((width, FF), lambda i: (0, 2))] * n_exp,
        out_specs=[
            pl.BlockSpec((step, width), lambda i: (jnp.minimum(i, half - 1), 0)),
            pl.BlockSpec((step, width), lambda i: (jnp.maximum(i - half, 0), 0)),
        ],
        compiler_params=pltpu.CompilerParams(vmem_limit_bytes=56 * 1024 * 1024),
        name="expert_value",
    )(*hidden, *works)


def expert_update(number, part, ups, downs, before):
    n_exp, up_rows, up_cols = ups[0].shape
    _, down_rows, down_cols = downs[0].shape
    steps = 4
    n_in = 6
    n_out = 8

    def body(up_part_ref, down_part_ref, *refs):
        ins = refs[:n_in]
        outs = refs[len(refs) - n_out :]
        grads = (
            up_part_ref[...].astype(jnp.float32),
            down_part_ref[...].astype(jnp.float32).T,
        )
        for which in range(2):
            weight, first, second = ins[3 * which : 3 * which + 3]
            grad = grads[which]
            new = adamw_update(weight[...], grad, first[...], second[...], WEIGHT_DECAY)
            outs[4 * which][...] = grad
            for place in range(3):
                outs[4 * which + 1 + place][...] = new[place]

    up_spec = pl.BlockSpec((None, up_rows // steps, up_cols), lambda i: (number, i, 0))
    down_spec = pl.BlockSpec((None, down_rows // steps, down_cols), lambda i: (number, i, 0))
    down_lane = down_rows // steps
    first_lane = up_cols // down_lane
    in_specs = [
        pl.BlockSpec((up_rows // steps, up_cols), lambda i: (i, 0)),
        pl.BlockSpec((up_rows, down_lane), lambda i: (0, first_lane + i)),
    ]
    in_specs += [up_spec] * 3 + [down_spec] * 3
    operands = [part, part, *ups, *downs]
    aliases = {}
    if before is not None:
        in_specs += [pl.BlockSpec(memory_space=pl.ANY)] * n_out
        aliases = {len(operands) + k: k for k in range(n_out)}
        operands += before
    return pl.pallas_call(
        body,
        grid=(steps,),
        out_shape=[jax.ShapeDtypeStruct(ups[0].shape, jnp.float32)] * 4
        + [jax.ShapeDtypeStruct(downs[0].shape, jnp.float32)] * 4,
        in_specs=in_specs,
        out_specs=[up_spec] * 4 + [down_spec] * 4,
        input_output_aliases=aliases,
        name="expert_update",
    )(*operands)


def local(
    hidden_in,
    out_cotangent,
    routes,
    route_probs,
    norm_gains,
    qkv_weight,
    out_weight,
    expert_up,
    expert_down,
    norm_gains_first,
    qkv_weight_first,
    out_weight_first,
    expert_up_first,
    expert_down_first,
    norm_gains_second,
    qkv_weight_second,
    out_weight_second,
    expert_up_second,
    expert_down_second,
):
    f32 = jnp.float32
    bf16 = jnp.bfloat16
    both = ("ctx", "fsdp")
    n_ctx = lax.axis_size("ctx")
    n_fsdp = lax.axis_size("fsdp")
    n_all = n_ctx * n_fsdp
    ctx_index = lax.axis_index("ctx")
    n_exp = expert_up.shape[0]
    shard = qkv_weight.shape[0]
    seq = DEVICE_TOKENS * n_ctx
    q_dev = QUERY_HEADS // n_ctx
    kv_dev = max(1, KEY_VALUE_HEADS // n_ctx)
    share = max(1, n_ctx // KEY_VALUE_HEADS)
    q_cols = q_dev * HEAD_SIZE
    kv_cols = kv_dev * HEAD_SIZE
    cols = q_cols + 2 * kv_cols

    tokens = hidden_in[0]
    cotangent = out_cotangent[0]

    expert_shards = [
        jnp.concatenate([expert_up[e].astype(bf16), expert_down[e].astype(bf16).T], 1)
        for e in range(n_exp)
    ]
    expert_shards[0], tokens = lax.optimization_barrier((expert_shards[0], tokens))
    expert_works = [lax.all_gather(part, "fsdp", axis=0, tiled=True) for part in expert_shards]
    inv_first = lax.rsqrt(jnp.mean(tokens * tokens, -1, keepdims=True) + NORM_EPS)
    unit_rows = (tokens * inv_first).astype(bf16)
    unit_all = gather_rows(unit_rows)

    gain_shard = norm_gains.astype(bf16).astype(f32)
    qkv_shard = qkv_weight.astype(bf16).astype(f32)
    scaled = (qkv_shard * gain_shard[0][:, None]).astype(bf16)
    q_part = scaled[:, :QUERY_FEATURES].reshape(shard, n_ctx, q_cols)
    k_part = scaled[:, QUERY_FEATURES : QUERY_FEATURES + KEY_FEATURES]
    v_part = scaled[:, QUERY_FEATURES + KEY_FEATURES :]
    k_part = jnp.repeat(k_part.reshape(shard, n_ctx // share, kv_cols), share, 1)
    v_part = jnp.repeat(v_part.reshape(shard, n_ctx // share, kv_cols), share, 1)
    head_cols = jnp.concatenate([q_part, k_part, v_part], -1).transpose(1, 0, 2)
    head_group = lax.all_to_all(head_cols, "ctx", split_axis=0, concat_axis=0, tiled=True)
    head_group = head_group.reshape(n_ctx * shard, cols)
    qkv_heads = assemble_heads(
        [head_group] + [exchange(head_group, "fsdp", mask) for mask in range(1, n_fsdp)], shard
    )

    gain_row = jnp.pad(norm_gains[1:2].astype(bf16), ((0, 7), (0, MODEL_WIDTH - shard)))
    out_shard = jnp.concatenate([out_weight.astype(bf16), gain_row], 0)
    out_group = [out_shard] + [exchange(out_shard, "fsdp", mask) for mask in range(1, n_fsdp)]

    experts = jnp.arange(n_exp * n_ctx, dtype=jnp.int32)
    chosen = routes[0][:, None, :] == experts[None, :, None]
    weight_rows = jnp.sum(jnp.where(chosen, route_probs[0][:, None, :], 0.0), 2).T
    weight_high = lax.reduce_precision(weight_rows, 8, 7)
    weight_low = weight_rows - weight_high
    weight_flat = jnp.stack([weight_high, weight_low]).reshape(-1, MODEL_WIDTH).astype(bf16)
    gain_flat = jnp.concatenate([part[shard : shard + 1, :shard] for part in out_group], 1)
    gain_flat = jnp.pad(gain_flat, ((0, 0), (0, MODEL_WIDTH - n_fsdp * shard)))
    n_misc = weight_flat.shape[0]
    misc_rows = -(-(n_misc + 1) // 16) * 16
    payload = jnp.concatenate(
        [
            (RES_SCALE * cotangent).astype(bf16),
            *[part[:shard] for part in out_group],
            weight_flat,
            gain_flat,
            jnp.zeros((misc_rows - n_misc - 1, MODEL_WIDTH), bf16),
        ],
        0,
    )

    def out_place(mask_fsdp):
        def place(k, mask, ctx, fsdp):
            return ((ctx ^ mask) * n_fsdp + (fsdp ^ mask_fsdp)) * shard

        return place

    payload_pieces = row_pieces(payload)

    moves = [(0, DEVICE_TOKENS, 0, lambda k, mask, ctx, fsdp: k * DEVICE_TOKENS)]
    for mask_fsdp in range(n_fsdp):
        moves.append((DEVICE_TOKENS + mask_fsdp * shard, shard, 1, out_place(mask_fsdp)))
    moves.append(
        (DEVICE_TOKENS + q_cols, misc_rows, 2, lambda k, mask, ctx, fsdp: k * misc_rows)
    )
    device_ids = ctx_index ^ jnp.array(relative_order(n_ctx), jnp.int32)
    row_ids = device_ids[:, None] * DEVICE_TOKENS + jnp.arange(DEVICE_TOKENS, dtype=jnp.int32)
    position = positions(row_ids.reshape(-1), DEVICE_TOKENS, n_ctx)
    cosine_table, sine_table = rope_tables(position, HEAD_SIZE)

    projected = jnp.dot(unit_all, qkv_heads, preferred_element_type=f32)
    query_heads = (
        apply_rotary(
            projected[:, :q_cols].reshape(seq, q_dev, HEAD_SIZE), cosine_table, sine_table
        )
        .astype(bf16)
        .reshape(seq, kv_dev, q_dev // kv_dev, HEAD_SIZE)
    )
    key_heads = apply_rotary(
        projected[:, q_cols : q_cols + kv_cols].reshape(seq, kv_dev, HEAD_SIZE),
        cosine_table,
        sine_table,
    ).astype(bf16)
    value_heads = projected[:, q_cols + kv_cols :].astype(bf16).reshape(seq, kv_dev, HEAD_SIZE)
    attended, logarithm_total = attend(query_heads, key_heads, value_heads, position, position)
    attended_rows = attended.reshape(seq, q_cols)
    attended_natural = reorder(attended_rows, n_ctx, True)
    attended_natural, payload_pieces = lax.optimization_barrier(
        (attended_natural, payload_pieces)
    )
    attn_rows = lax.all_to_all(attended_natural, "ctx", 0, 0, tiled=True)
    cotangent_all, out_all, misc_all = assemble(
        payload_pieces, [seq, MODEL_WIDTH, n_ctx * misc_rows], moves
    )
    misc_all = misc_all.reshape(n_ctx, misc_rows, MODEL_WIDTH)
    weight_all = (
        misc_all[:, :n_misc]
        .astype(f32)
        .reshape(n_ctx, 2, n_exp * n_ctx, DEVICE_TOKENS)
    )
    weight_all = lax.dynamic_slice_in_dim(
        weight_all[:, 0] + weight_all[:, 1], ctx_index * n_exp, n_exp, 1
    )
    weight_own = weight_all.transpose(0, 2, 1).reshape(seq, n_exp)
    gain_pieces = misc_all[:, n_misc, : n_fsdp * shard].astype(f32)
    group_ids = lax.axis_index("fsdp") ^ jnp.arange(n_fsdp, dtype=jnp.int32)
    piece_ids = (device_ids[:, None] * n_fsdp + group_ids[None, :]).reshape(n_all)
    is_piece = piece_ids[None, :] == jnp.arange(n_all, dtype=jnp.int32)[:, None]
    gain_ffn = jnp.sum(
        jnp.where(is_piece[:, :, None], gain_pieces.reshape(1, n_all, shard), 0.0), 1
    ).reshape(1, MODEL_WIDTH)

    residual, normed_ffn = project_out(attn_rows, out_all, tokens, gain_ffn)

    normed_all = gather_rows(normed_ffn)
    hidden = []
    expert_rows = []
    sums = [None]
    half = seq // 2
    for e in range(n_exp):
        weighted_hidden, pair_grad, *sums = expert_front(
            normed_all, cotangent_all, expert_works[e], weight_own[:, e : e + 1], sums[0]
        )
        if e == n_exp - 1:
            own_grad, grad_parts = pair_parts(*sums)
            grad_parts, weighted_hidden, pair_grad = lax.optimization_barrier(
                (grad_parts, weighted_hidden, pair_grad)
            )
            other_grads = send_parts(grad_parts)
        hidden.append(weighted_hidden)
        expert_term = expert_grads(normed_all, pair_grad, cotangent_all, weighted_hidden)
        if e < n_exp - 1:
            expert_works[e + 1], expert_term = lax.optimization_barrier(
                (expert_works[e + 1], expert_term)
            )
        expert_part = lax.psum_scatter(expert_term, "fsdp", scatter_dimension=0, tiled=True)
        expert_rows.append(with_layout_constraint(expert_part, Layout(major_to_minor=(0, 1))))
    value_sums = expert_value(hidden, expert_works)
    own_grad, value_sums = lax.optimization_barrier((own_grad, value_sums))

    residual_grad, attn_grad, gain_ffn_part, head_grads = residual_back(
        own_grad, other_grads, residual, cotangent, gain_ffn, out_all
    )
    gain_ffn_part = gain_ffn_part[0]
    hidden_out = residual + RES_SCALE * scatter_sum(*value_sums)
    attn_out_heads = reorder(
        lax.all_to_all(head_grads, "ctx", 0, 0, tiled=True), n_ctx, False
    )
    query_gradient, key_gradient, value_gradient = attend_back(
        query_heads,
        key_heads,
        value_heads,
        attended,
        attn_out_heads.reshape(seq, kv_dev, q_dev // kv_dev, HEAD_SIZE),
        logarithm_total,
        position,
        position,
    )
    query_rows = inverse_rotary(
        query_gradient.reshape(seq, q_dev, HEAD_SIZE), cosine_table, sine_table
    )
    key_rows = inverse_rotary(key_gradient, cosine_table, sine_table)
    qkv_rows = jnp.concatenate(
        [
            query_rows.reshape(seq, q_cols),
            key_rows.reshape(seq, kv_cols),
            value_gradient.reshape(seq, kv_cols),
        ],
        1,
    ).astype(bf16)
    grad_all = gather_rows(attn_grad)
    out_term = lax.dot_general(
        attended_rows, grad_all, (((0,), (0,)), ((), ())), preferred_element_type=f32
    ).astype(bf16)
    out_term, qkv_rows = lax.optimization_barrier((out_term, qkv_rows))

    def in_grad_rows(rows):
        return lax.dot_general(
            rows, qkv_heads, (((1,), (1,)), ((), ())), preferred_element_type=f32
        )

    odd_in_grad = in_grad_rows(qkv_rows[half:]).astype(bf16)
    scaled_in_grad, in_parts = pair_parts(in_grad_rows(qkv_rows[:half]), odd_in_grad)
    in_parts, qkv_rows = lax.optimization_barrier((in_parts, qkv_rows))
    in_received = send_parts(in_parts)

    def update_expert(e, updates):
        return expert_update(
            e,
            expert_rows[e],
            (expert_up, expert_up_first, expert_up_second),
            (expert_down, expert_down_first, expert_down_second),
            updates,
        )

    updates = None
    for e in range(n_exp - 1):
        updates = update_expert(e, updates)
    scaled_in_grad = scaled_in_grad + in_received[0].astype(f32)
    updates, scaled_in_grad = lax.optimization_barrier((updates, scaled_in_grad))
    for part in in_received[1:]:
        scaled_in_grad = scaled_in_grad + part.astype(f32)
    input_grad = (
        residual_grad
        + inv_first * scaled_in_grad
        - tokens * inv_first**3 * jnp.mean(scaled_in_grad * tokens, -1, keepdims=True)
    )

    fsdp_index = lax.axis_index("fsdp")

    def out_block(mask):
        return lax.dynamic_slice_in_dim(out_term, (fsdp_index ^ mask) * shard, shard, 0)

    out_grad = out_block(0).astype(f32)
    for mask in range(1, n_fsdp):
        out_grad = out_grad + exchange(out_block(mask), "fsdp", mask).astype(f32)
    qkv_term = lax.dot_general(
        unit_all, qkv_rows, (((0,), (0,)), ((), ())), preferred_element_type=f32
    ).astype(bf16)
    gain_high = lax.reduce_precision(gain_ffn_part, 8, 7)
    gain_parts = jnp.stack([gain_high, gain_ffn_part - gain_high]).reshape(2, n_all, shard)
    gain_parts = jnp.pad(
        gain_parts.transpose(1, 0, 2).astype(bf16), ((0, 0), (0, 6), (0, cols - shard))
    )
    qkv_pieces = lax.all_to_all(
        jnp.concatenate([qkv_term.reshape(n_all, shard, cols), gain_parts], 1),
        both,
        0,
        0,
        tiled=True,
    ).reshape(n_ctx, n_fsdp, shard + 8, cols)
    gain_ffn_grad = jnp.sum(qkv_pieces[:, :, shard : shard + 2, :shard].astype(f32), (0, 1, 2))
    qkv_pieces = qkv_pieces[:, :, :shard]
    qkv_sum = jnp.sum(qkv_pieces.astype(f32), 1)
    kv_sum = jnp.sum(
        qkv_sum[..., q_cols:].reshape(n_ctx // share, share, shard, 2, kv_cols), 1
    ).transpose(1, 2, 0, 3)
    unit_grad = jnp.concatenate(
        [
            qkv_sum[..., :q_cols].transpose(1, 0, 2).reshape(shard, QUERY_FEATURES),
            kv_sum.reshape(shard, 2 * KEY_FEATURES),
        ],
        1,
    )
    qkv_grad = gain_shard[0][:, None] * unit_grad
    gain_attn_grad = jnp.sum(qkv_shard * unit_grad, 1)
    gains_grad = jnp.stack([gain_attn_grad, gain_ffn_grad])

    norm_new = adamw_update(norm_gains, gains_grad, norm_gains_first, norm_gains_second, 0.0)
    qkv_new = adamw_update(qkv_weight, qkv_grad, qkv_weight_first, qkv_weight_second, WEIGHT_DECAY)
    out_new = adamw_update(out_weight, out_grad, out_weight_first, out_weight_second, WEIGHT_DECAY)
    updates = update_expert(n_exp - 1, updates)
    up_grad_shard, *up_new = updates[:4]
    down_grad_shard, *down_new = updates[4:]
    return (
        hidden_out[None],
        input_grad[None],
        gains_grad,
        qkv_grad,
        out_grad,
        up_grad_shard,
        down_grad_shard,
        norm_new[0],
        qkv_new[0],
        out_new[0],
        up_new[0],
        down_new[0],
        norm_new[1],
        qkv_new[1],
        out_new[1],
        up_new[1],
        down_new[1],
        norm_new[2],
        qkv_new[2],
        out_new[2],
        up_new[2],
        down_new[2],
    )


def solution(mesh):
    in_specs = (
        P("fsdp", "ctx", None),
        P("fsdp", "ctx", None),
        P("fsdp", "ctx", None),
        P("fsdp", "ctx", None),
        P(None, ("ctx", "fsdp")),
        P(("ctx", "fsdp"), None),
        P(("ctx", "fsdp"), None),
        P("ctx", "fsdp", None),
        P("ctx", None, "fsdp"),
        P(None, ("ctx", "fsdp")),
        P(("ctx", "fsdp"), None),
        P(("ctx", "fsdp"), None),
        P("ctx", "fsdp", None),
        P("ctx", None, "fsdp"),
        P(None, ("ctx", "fsdp")),
        P(("ctx", "fsdp"), None),
        P(("ctx", "fsdp"), None),
        P("ctx", "fsdp", None),
        P("ctx", None, "fsdp"),
    )
    out_specs = (
        P("fsdp", "ctx", None),
        P("fsdp", "ctx", None),
        P(None, ("ctx", "fsdp")),
        P(("ctx", "fsdp"), None),
        P(("ctx", "fsdp"), None),
        P("ctx", "fsdp", None),
        P("ctx", None, "fsdp"),
        P(None, ("ctx", "fsdp")),
        P(("ctx", "fsdp"), None),
        P(("ctx", "fsdp"), None),
        P("ctx", "fsdp", None),
        P("ctx", None, "fsdp"),
        P(None, ("ctx", "fsdp")),
        P(("ctx", "fsdp"), None),
        P(("ctx", "fsdp"), None),
        P("ctx", "fsdp", None),
        P("ctx", None, "fsdp"),
        P(None, ("ctx", "fsdp")),
        P(("ctx", "fsdp"), None),
        P(("ctx", "fsdp"), None),
        P("ctx", "fsdp", None),
        P("ctx", None, "fsdp"),
    )
    return jax.shard_map(local, mesh=mesh, in_specs=in_specs, out_specs=out_specs, check_vma=False)
```

```python
import jax
import jax.numpy as jnp
from jax import lax
from jax.experimental import pallas as pl
from jax.experimental.layout import Layout, with_layout_constraint
from jax.experimental.pallas import tpu as pltpu
from jax.sharding import PartitionSpec as P

MODEL_WIDTH = 1024
QUERY_HEADS = 16
KEY_VALUE_HEADS = 8
HEAD_SIZE = 64
FF = 512
DEVICE_TOKENS = 128
QUERY_FEATURES = 1024
KEY_FEATURES = 512


RES_SCALE = 0.22
SCORE_SCALE = 0.015625
NORM_EPS = 1e-06
ROPE_BASE = 10000.0
LEARN_RATE = 0.02
BETA_FIRST = 0.9
BETA_SECOND = 0.999
ADAM_EPS = 1e-08
WEIGHT_DECAY = 0.1
ADAM_STEP = 3.0
MASK_VALUE = -1e30
EXPERT_STEP = 256


def positions(row_ids, tok_dev, n_ctx):
    device = row_ids // tok_dev
    within = row_ids % tok_dev
    half_block = tok_dev // 2
    return jnp.where(
        within < half_block,
        device * half_block + within,
        (2 * n_ctx - 1 - device) * half_block + within - half_block,
    )


def rope_tables(position):
    lane = jnp.arange(2 * HEAD_SIZE, dtype=jnp.int32)
    half_dim = HEAD_SIZE // 2
    frequency = ROPE_BASE ** (-((lane % half_dim).astype(jnp.float32) * 2.0 / HEAD_SIZE))
    angles = position.astype(jnp.float32)[:, None] * frequency[None, :]
    cosine, sine = jnp.cos(angles), jnp.sin(angles)
    is_key = (lane < HEAD_SIZE)[None, :]
    return cosine, sine, jnp.where(is_key, cosine, 1.0), jnp.where(is_key, sine, 0.0)


def adamw_update(weight, gradient, first_moment, second_moment, decay_rate):
    first_new = BETA_FIRST * first_moment + (1.0 - BETA_FIRST) * gradient
    second_new = BETA_SECOND * second_moment + (1.0 - BETA_SECOND) * gradient * gradient
    first_hat = first_new / (1.0 - BETA_FIRST**ADAM_STEP)
    second_hat = second_new / (1.0 - BETA_SECOND**ADAM_STEP)
    weight_new = weight - LEARN_RATE * (
        first_hat / (jnp.sqrt(second_hat) + ADAM_EPS) + decay_rate * weight
    )
    return (weight_new, first_new, second_new)


def cost(micros):
    return pl.CostEstimate(flops=int(micros * 1e9), bytes_accessed=1 << 20, transcendentals=0)


def xor_perm(size, mask):
    return [(i, i ^ mask) for i in range(size)]


def exchange(values, axis, mask):
    return lax.ppermute(values, axis, xor_perm(lax.axis_size(axis), mask))


def relative_order(size):
    return list(range(0, size, 2)) + list(range(1, size, 2))


def assemble(pieces, sizes, moves):
    count = len(pieces)
    order = relative_order(count)

    def body(index_ref, *refs):
        outs = refs[count : count + len(sizes)]
        copies = []
        for k in range(count):
            for m, (start, length, number, place) in enumerate(moves):
                at = place(k, order[k], index_ref[0], index_ref[1])
                if not isinstance(at, int):
                    at = pl.multiple_of(at, length)
                copies.append(
                    pltpu.make_async_copy(
                        refs[k].at[pl.ds(start, length)],
                        outs[number].at[pl.ds(at, length)],
                        refs[-1].at[k, m],
                    )
                )
        for copy in copies:
            copy.start()
        for copy in copies:
            copy.wait()

    width = pieces[0].shape[1]
    return pl.pallas_call(
        body,
        out_shape=[jax.ShapeDtypeStruct((size, width), pieces[0].dtype) for size in sizes],
        in_specs=[pl.BlockSpec(memory_space=pltpu.SMEM)]
        + [pl.BlockSpec(memory_space=pl.ANY)] * count,
        out_specs=[pl.BlockSpec(memory_space=pltpu.VMEM)] * len(sizes),
        scratch_shapes=[pltpu.SemaphoreType.DMA((count, len(moves)))],
        name="assemble",
    )(jnp.concatenate([device_index("ctx"), device_index("fsdp")]), *pieces)


def assemble_heads(pieces, shard):
    size = len(pieces)
    rows, cols = pieces[0].shape
    count = rows // shard

    def body(index_ref, *refs):
        copies = []
        for mask in range(size):
            for i in range(count):
                at = pl.multiple_of((i * size + (index_ref[0] ^ mask)) * shard, shard)
                copies.append(
                    pltpu.make_async_copy(
                        refs[mask].at[pl.ds(i * shard, shard)],
                        refs[size].at[pl.ds(at, shard)],
                        refs[-1].at[mask, i],
                    )
                )
        for copy in copies:
            copy.start()
        for copy in copies:
            copy.wait()

    return pl.pallas_call(
        body,
        out_shape=jax.ShapeDtypeStruct((rows * size, cols), pieces[0].dtype),
        in_specs=[pl.BlockSpec(memory_space=pltpu.SMEM)]
        + [pl.BlockSpec(memory_space=pl.ANY)] * size,
        out_specs=pl.BlockSpec(memory_space=pltpu.VMEM),
        scratch_shapes=[pltpu.SemaphoreType.DMA((size, count))],
        name="assemble_heads",
    )(device_index("fsdp"), *pieces)


def device_index(axis):
    return lax.axis_index(axis).astype(jnp.int32).reshape(1)


def project_out(heads, out_all, tokens, gain):
    count = heads.shape[0] // tokens.shape[0]
    length, width = tokens.shape
    cols = heads.shape[1]

    def body(heads_ref, out_ref, tokens_ref, gain_ref, residual_ref, normed_ref):
        total = jnp.zeros((length, width), jnp.float32)
        for place in range(count):
            total = total + jnp.dot(
                heads_ref[place * length : (place + 1) * length, :],
                out_ref[place * cols : (place + 1) * cols, :],
                preferred_element_type=jnp.float32,
            )
        residual = tokens_ref[...] + RES_SCALE * total
        inv = lax.rsqrt(jnp.mean(residual * residual, -1, keepdims=True) + NORM_EPS)
        residual_ref[...] = residual
        normed_ref[...] = (residual * inv * gain_ref[...]).astype(jnp.bfloat16)

    vmem = pl.BlockSpec(memory_space=pltpu.VMEM)
    return pl.pallas_call(
        body,
        out_shape=[
            jax.ShapeDtypeStruct((length, width), jnp.float32),
            jax.ShapeDtypeStruct((length, width), jnp.bfloat16),
        ],
        in_specs=[vmem] * 4,
        out_specs=[vmem] * 2,
        name="project_out",
    )(heads, out_all, tokens, gain)


def residual_back(own, received, residual, cotangent, gain, out_all):
    length, width = residual.shape
    count = lax.axis_size("ctx")
    cols = out_all.shape[0] // count
    n_parts = len(received)

    def body(own_ref, *refs):
        parts = refs[:n_parts]
        residual_ref, cotangent_ref, gain_ref, out_ref = refs[n_parts : n_parts + 4]
        grad_ref, attn_ref, gain_grad_ref, heads_ref = refs[n_parts + 4 :]
        ffn_grad = own_ref[...]
        for part in parts:
            ffn_grad = ffn_grad + part[...].astype(jnp.float32)
        rows = residual_ref[...]
        inv = lax.rsqrt(jnp.mean(rows * rows, -1, keepdims=True) + NORM_EPS)
        weighted = gain_ref[...] * ffn_grad
        gain_grad_ref[...] = jnp.sum(ffn_grad * rows * inv, 0, keepdims=True)
        grad = (
            cotangent_ref[...]
            + inv * weighted
            - rows * (inv * inv * inv) * jnp.mean(weighted * rows, -1, keepdims=True)
        )
        grad_ref[...] = grad
        attn_grad = (RES_SCALE * grad).astype(jnp.bfloat16)
        attn_ref[...] = attn_grad
        for place in range(count):
            heads_ref[place * length : (place + 1) * length, :] = lax.dot_general(
                attn_grad,
                out_ref[place * cols : (place + 1) * cols, :],
                (((1,), (1,)), ((), ())),
                preferred_element_type=jnp.float32,
            ).astype(jnp.bfloat16)

    vmem = pl.BlockSpec(memory_space=pltpu.VMEM)
    return pl.pallas_call(
        body,
        out_shape=[
            jax.ShapeDtypeStruct((length, width), jnp.float32),
            jax.ShapeDtypeStruct((length, width), jnp.bfloat16),
            jax.ShapeDtypeStruct((1, width), jnp.float32),
            jax.ShapeDtypeStruct((count * length, cols), jnp.bfloat16),
        ],
        in_specs=[vmem] * (5 + n_parts),
        out_specs=[vmem] * 4,
        name="residual_back",
    )(own, *received, residual, cotangent, gain, out_all)


def row_pieces(rows):
    size = lax.axis_size("ctx")
    even = [rows] + [exchange(rows, "ctx", mask) for mask in range(2, size, 2)]
    return even + [exchange(piece, "ctx", 1) for piece in even]


def gather_rows(rows, natural=False):
    length = rows.shape[0]
    pieces = row_pieces(rows)

    def place(k, mask, ctx, fsdp):
        return (ctx ^ mask) * length if natural else k * length

    move = (0, length, 0, place)
    return assemble(pieces, [length * len(pieces)], [move])[0]


def pair_parts(even_rows, odd_rows):
    size = lax.axis_size("ctx")
    block = even_rows.shape[0] * 2 // size
    pair_sum = even_rows + exchange(odd_rows, "ctx", 1).astype(jnp.float32)
    parts = [
        pair_sum[place * block : (place + 1) * block].astype(jnp.bfloat16)
        for place in range(1, size // 2)
    ]
    return pair_sum[:block], parts


def send_parts(parts):
    return [exchange(part, "ctx", 2 * place + 2) for place, part in enumerate(parts)]


def scatter_sum(even_rows, odd_rows):
    total, parts = pair_parts(even_rows, odd_rows)
    for part in send_parts(parts):
        total = total + part.astype(jnp.float32)
    return total


def expert_front(normed_all, cotangent_all, work, weight, before):
    seq, width = normed_all.shape
    step = EXPERT_STEP
    steps = seq // step
    half = steps // 2
    last = before is not None

    def body(rows_ref, back_ref, work_ref, weight_ref, *refs):
        if last:
            before_ref, hidden_ref, pair_ref, even_ref, odd_ref = refs
        else:
            hidden_ref, pair_ref, even_ref = refs
        gate_up = jnp.dot(rows_ref[...], work_ref[:, : 2 * FF], preferred_element_type=jnp.float32)
        gate = gate_up[:, :FF]
        up = gate_up[:, FF:]
        sig = 1.0 / (1.0 + jnp.exp(-gate))
        act = gate * sig
        hidden_ref[...] = (weight_ref[...] * (act * up)).astype(jnp.bfloat16)
        back = weight_ref[...] * jnp.dot(
            back_ref[...], work_ref[:, 2 * FF :], preferred_element_type=jnp.float32
        )
        pair_ref[:, :FF] = (back * up * sig * (1.0 + gate * (1.0 - sig))).astype(jnp.bfloat16)
        pair_ref[:, FF:] = (back * act).astype(jnp.bfloat16)
        total = lax.dot_general(
            pair_ref[...],
            work_ref[:, : 2 * FF],
            (((1,), (1,)), ((), ())),
            preferred_element_type=jnp.float32,
        )
        if not last:
            even_ref[...] = total
        else:
            total = total + before_ref[...]

            @pl.when(pl.program_id(0) < half)
            def _():
                even_ref[...] = total

            @pl.when(pl.program_id(0) >= half)
            def _():
                odd_ref[...] = total.astype(jnp.bfloat16)

    rows_spec = pl.BlockSpec((step, width), lambda i: (i, 0))
    out_shape = [
        jax.ShapeDtypeStruct((seq, FF), jnp.bfloat16),
        jax.ShapeDtypeStruct((seq, 2 * FF), jnp.bfloat16),
    ]
    out_specs = [
        pl.BlockSpec((step, FF), lambda i: (i, 0)),
        pl.BlockSpec((step, 2 * FF), lambda i: (i, 0)),
    ]
    if last:
        out_shape += [
            jax.ShapeDtypeStruct((seq // 2, width), jnp.float32),
            jax.ShapeDtypeStruct((seq // 2, width), jnp.bfloat16),
        ]
        out_specs += [
            pl.BlockSpec((step, width), lambda i: (jnp.minimum(i, half - 1), 0)),
            pl.BlockSpec((step, width), lambda i: (jnp.maximum(i - half, 0), 0)),
        ]
    else:
        out_shape.append(jax.ShapeDtypeStruct((seq, width), jnp.float32))
        out_specs.append(rows_spec)
    return pl.pallas_call(
        body,
        grid=(steps,),
        out_shape=out_shape,
        in_specs=[
            rows_spec,
            rows_spec,
            pl.BlockSpec(work.shape, lambda i: (0, 0)),
            pl.BlockSpec((step, 1), lambda i: (i, 0)),
        ]
        + [rows_spec] * last,
        out_specs=out_specs,
        compiler_params=pltpu.CompilerParams(vmem_limit_bytes=56 * 1024 * 1024),
        cost_estimate=cost(11),
        name="expert_front",
    )(normed_all, cotangent_all, work, weight, *([before] * last))


def expert_grads(normed_all, pair_grad, cotangent_all, hidden):
    seq, width = normed_all.shape
    step = 256

    def body(rows_ref, pair_ref, back_ref, hidden_ref, out_ref):
        contract = (((0,), (0,)), ((), ()))
        out_ref[:, : 2 * FF] = lax.dot_general(
            rows_ref[...], pair_ref[...], contract, preferred_element_type=jnp.float32
        ).astype(jnp.bfloat16)
        out_ref[:, 2 * FF :] = lax.dot_general(
            back_ref[...], hidden_ref[...], contract, preferred_element_type=jnp.float32
        ).astype(jnp.bfloat16)

    cols_spec = pl.BlockSpec((seq, step), lambda i: (0, i))
    return pl.pallas_call(
        body,
        grid=(width // step,),
        out_shape=jax.ShapeDtypeStruct((width, 3 * FF), jnp.bfloat16),
        in_specs=[
            cols_spec,
            pl.BlockSpec(pair_grad.shape, lambda i: (0, 0)),
            cols_spec,
            pl.BlockSpec(hidden.shape, lambda i: (0, 0)),
        ],
        out_specs=pl.BlockSpec((step, 3 * FF), lambda i: (i, 0)),
        compiler_params=pltpu.CompilerParams(vmem_limit_bytes=56 * 1024 * 1024),
        cost_estimate=cost(8),
        name="expert_grads",
    )(normed_all, pair_grad, cotangent_all, hidden)


def expert_value(hidden, works):
    seq = hidden[0].shape[0]
    n_exp = len(works)
    width = works[0].shape[0]
    step = EXPERT_STEP
    half = seq // step // 2

    def body(*refs):
        even_ref, odd_ref = refs[2 * n_exp :]
        total = jnp.zeros((step, width), jnp.float32)
        for e in range(n_exp):
            total = total + lax.dot_general(
                refs[e][...],
                refs[n_exp + e][...],
                (((1,), (1,)), ((), ())),
                preferred_element_type=jnp.float32,
            )

        @pl.when(pl.program_id(0) < half)
        def _():
            even_ref[...] = total

        @pl.when(pl.program_id(0) >= half)
        def _():
            odd_ref[...] = total.astype(jnp.bfloat16)

    return pl.pallas_call(
        body,
        grid=(seq // step,),
        out_shape=[
            jax.ShapeDtypeStruct((seq // 2, width), jnp.float32),
            jax.ShapeDtypeStruct((seq // 2, width), jnp.bfloat16),
        ],
        in_specs=[pl.BlockSpec((step, FF), lambda i: (i, 0))] * n_exp
        + [pl.BlockSpec((width, FF), lambda i: (0, 2))] * n_exp,
        out_specs=[
            pl.BlockSpec((step, width), lambda i: (jnp.minimum(i, half - 1), 0)),
            pl.BlockSpec((step, width), lambda i: (jnp.maximum(i - half, 0), 0)),
        ],
        compiler_params=pltpu.CompilerParams(vmem_limit_bytes=56 * 1024 * 1024),
        cost_estimate=cost(6.5),
        name="expert_value",
    )(*hidden, *works)


def expert_update(number, part, ups, downs, before):
    _, up_rows, up_cols = ups[0].shape
    _, down_rows, down_cols = downs[0].shape
    steps = 4
    n_in = 6
    n_out = 8

    def body(up_part_ref, down_part_ref, *refs):
        ins = refs[:n_in]
        outs = refs[len(refs) - n_out :]
        grads = (
            up_part_ref[...].astype(jnp.float32),
            down_part_ref[...].astype(jnp.float32).T,
        )
        for which in range(2):
            weight, first, second = ins[3 * which : 3 * which + 3]
            grad = grads[which]
            new = adamw_update(weight[...], grad, first[...], second[...], WEIGHT_DECAY)
            outs[4 * which][...] = grad
            for place in range(3):
                outs[4 * which + 1 + place][...] = new[place]

    up_spec = pl.BlockSpec((None, up_rows // steps, up_cols), lambda i: (number, i, 0))
    down_spec = pl.BlockSpec((None, down_rows // steps, down_cols), lambda i: (number, i, 0))
    down_lane = down_rows // steps
    first_lane = up_cols // down_lane
    in_specs = [
        pl.BlockSpec((up_rows // steps, up_cols), lambda i: (i, 0)),
        pl.BlockSpec((up_rows, down_lane), lambda i: (0, first_lane + i)),
    ]
    in_specs += [up_spec] * 3 + [down_spec] * 3
    operands = [part, part, *ups, *downs]
    aliases = {}
    if before is not None:
        in_specs += [pl.BlockSpec(memory_space=pl.ANY)] * n_out
        aliases = {len(operands) + k: k for k in range(n_out)}
        operands += before
    return pl.pallas_call(
        body,
        grid=(steps,),
        out_shape=[jax.ShapeDtypeStruct(ups[0].shape, jnp.float32)] * 4
        + [jax.ShapeDtypeStruct(downs[0].shape, jnp.float32)] * 4,
        in_specs=in_specs,
        out_specs=[up_spec] * 4 + [down_spec] * 4,
        input_output_aliases=aliases,
        cost_estimate=cost(6.4),
        name="expert_update",
    )(*operands)


def spin(values, cosine, sine, back):
    lane = lax.broadcasted_iota(jnp.int32, values.shape, 1)
    lower = (lane % HEAD_SIZE) < HEAD_SIZE // 2
    width = values.shape[1]
    from_upper = pltpu.roll(values, width - HEAD_SIZE // 2, 1)
    from_lower = pltpu.roll(values, HEAD_SIZE // 2, 1)
    turned = jnp.where(lower, from_upper, from_lower) * sine
    if back:
        turned = -turned
    return values * cosine + jnp.where(lower, -turned, turned)


def head_tiles(kv_rows):
    lane = lax.broadcasted_iota(jnp.int32, kv_rows.shape, 1)
    swapped = pltpu.roll(kv_rows.astype(jnp.float32), HEAD_SIZE, 1).astype(kv_rows.dtype)
    zero = jnp.zeros_like(kv_rows)
    return jnp.where(lane < HEAD_SIZE, kv_rows, zero), jnp.where(lane < HEAD_SIZE, swapped, kv_rows)


def attention(unit_all, qkv_heads, tables, position, n_heads, n_ctx):
    seq = unit_all.shape[0]
    step = DEVICE_TOKENS
    order = relative_order(n_ctx)
    wide = 2 * HEAD_SIZE

    def body(
        slot_ref, rows_ref, work_ref, cosine_ref, sine_ref, kv_cos_ref, kv_sin_ref,
        column_ref, row_ref, query_ref, kv_ref, heads_ref, total_ref,
    ):
        def project(i, carry):
            at = pl.ds(pl.multiple_of(i * 256, 256), 256)
            out = jnp.dot(rows_ref[at, :], work_ref[...], preferred_element_type=jnp.float32)
            query_ref[at, :] = spin(
                out[:, :wide], cosine_ref[at, :], sine_ref[at, :], False
            ).astype(jnp.bfloat16)
            kv_ref[at, :] = spin(
                out[:, wide:], kv_cos_ref[at, :], kv_sin_ref[at, :], False
            ).astype(jnp.bfloat16)
            return carry

        lax.fori_loop(0, seq // 256, project, 0)
        keys, values = head_tiles(kv_ref[...])
        lane = lax.broadcasted_iota(jnp.int32, (step, wide), 1)

        def attend_block(i, carry):
            at = pl.ds(pl.multiple_of(i * step, step), step)
            allowed = row_ref[...] <= column_ref[at, :]
            queries = query_ref[at, :].astype(jnp.float32)
            out = jnp.zeros((step, wide), jnp.float32)
            totals = jnp.zeros((step, wide), jnp.float32)
            for head in range(n_heads):
                mine = queries if head == 0 else pltpu.roll(queries, HEAD_SIZE, 1)
                scores = lax.dot_general(
                    mine.astype(jnp.bfloat16), keys, (((1,), (1,)), ((), ())),
                    preferred_element_type=jnp.float32,
                )
                scores = jnp.where(allowed, scores * SCORE_SCALE, MASK_VALUE)
                top = jnp.max(scores, -1, keepdims=True)
                total = top + jnp.log(jnp.sum(jnp.exp(scores - top), -1, keepdims=True))
                probs = jnp.exp(scores - total).astype(jnp.bfloat16)
                got = jnp.dot(probs, values, preferred_element_type=jnp.float32)
                is_mine = (lane >= head * HEAD_SIZE) & (lane < (head + 1) * HEAD_SIZE)
                out = jnp.where(is_mine, got, out)
                totals = jnp.where(is_mine, total, totals)
            there = pl.multiple_of(slot_ref[i] * step, step)
            heads_ref[pl.ds(there, step), :] = out.astype(jnp.bfloat16)
            total_ref[at, :] = totals
            return carry

        lax.fori_loop(0, seq // step, attend_block, 0)

    vmem = pl.BlockSpec(memory_space=pltpu.VMEM)
    slots = device_index("ctx") ^ jnp.array(order, jnp.int32)
    return pl.pallas_call(
        body,
        out_shape=[
            jax.ShapeDtypeStruct((seq, wide), jnp.bfloat16),
            jax.ShapeDtypeStruct((seq, wide), jnp.bfloat16),
            jax.ShapeDtypeStruct((seq, wide), jnp.bfloat16),
            jax.ShapeDtypeStruct((seq, wide), jnp.float32),
        ],
        in_specs=[pl.BlockSpec(memory_space=pltpu.SMEM)] + [vmem] * 8,
        out_specs=[vmem] * 4,
        compiler_params=pltpu.CompilerParams(vmem_limit_bytes=56 * 1024 * 1024),
        cost_estimate=cost(14),
        name="attention",
    )(slots, unit_all, qkv_heads, *tables, position[:, None], position[None, :])


def attention_back(query, kv, heads, head_grads, totals, tables, position, n_heads, n_ctx):
    seq = query.shape[0]
    step = DEVICE_TOKENS
    order = relative_order(n_ctx)
    wide = 2 * HEAD_SIZE

    def body(
        slot_ref, query_ref, kv_ref, heads_ref, grads_ref, total_ref, cosine_ref, sine_ref,
        kv_cos_ref, kv_sin_ref, row_ref, column_ref, out_ref, sum_ref,
    ):
        keys, values = head_tiles(kv_ref[...])
        lane = lax.broadcasted_iota(jnp.int32, (seq, wide), 1)
        values = jnp.where(lane < HEAD_SIZE, values, jnp.zeros_like(values))
        keys_turned = keys.astype(jnp.float32).T.astype(jnp.bfloat16)
        sum_ref[...] = jnp.zeros_like(sum_ref)
        low = lax.broadcasted_iota(jnp.int32, (step, wide), 1) < HEAD_SIZE

        def block(i, carry):
            at = pl.ds(pl.multiple_of(i * step, step), step)
            there = pl.ds(pl.multiple_of(slot_ref[i] * step, step), step)
            queries = query_ref[at, :].astype(jnp.float32)
            grads = grads_ref[there, :].astype(jnp.float32)
            dots = grads * heads_ref[there, :].astype(jnp.float32)
            totals = total_ref[at, :]
            allowed = column_ref[...] <= row_ref[:, at]
            parts = []
            for head in range(n_heads):
                if head:
                    queries = pltpu.roll(queries, HEAD_SIZE, 1)
                    grads = pltpu.roll(grads, HEAD_SIZE, 1)
                    dots = pltpu.roll(dots, HEAD_SIZE, 1)
                    totals = pltpu.roll(totals, HEAD_SIZE, 1)
                mine = jnp.where(low, queries, 0.0).astype(jnp.bfloat16)
                grad = jnp.where(low, grads, 0.0)
                grad_high = pltpu.roll(grad, HEAD_SIZE, 1).astype(jnp.bfloat16)
                grad = grad.astype(jnp.bfloat16)
                row_dot = jnp.sum(jnp.where(low, dots, 0.0), -1, keepdims=True)
                row_dot = jnp.broadcast_to(row_dot, (step, wide)).T[:1, :]
                total = totals.T[:1, :]
                scores = lax.dot_general(
                    keys, mine, (((1,), (1,)), ((), ())), preferred_element_type=jnp.float32
                )
                scores = jnp.where(allowed, scores * SCORE_SCALE, MASK_VALUE)
                probs = jnp.exp(scores - total)
                prob_grad = lax.dot_general(
                    values, grad, (((1,), (1,)), ((), ())), preferred_element_type=jnp.float32
                )
                score_grad = (probs * (prob_grad - row_dot) * SCORE_SCALE).astype(jnp.bfloat16)
                sum_ref[...] += jnp.dot(
                    score_grad, mine, preferred_element_type=jnp.float32
                ) + jnp.dot(
                    probs.astype(jnp.bfloat16), grad_high, preferred_element_type=jnp.float32
                )
                parts.append(
                    jnp.dot(
                        keys_turned[:HEAD_SIZE, :], score_grad, preferred_element_type=jnp.float32
                    )
                )
            while len(parts) < 2:
                parts.append(jnp.zeros_like(parts[0]))
            query_grad = jnp.concatenate(parts, 0).T
            out_ref[at, :wide] = spin(
                query_grad, cosine_ref[at, :], sine_ref[at, :], True
            ).astype(jnp.bfloat16)
            return carry

        lax.fori_loop(0, seq // step, block, 0)

        def finish(i, carry):
            at = pl.ds(pl.multiple_of(i * step, step), step)
            out_ref[at, wide:] = spin(
                sum_ref[at, :], kv_cos_ref[at, :], kv_sin_ref[at, :], True
            ).astype(jnp.bfloat16)
            return carry

        lax.fori_loop(0, seq // step, finish, 0)

    vmem = pl.BlockSpec(memory_space=pltpu.VMEM)
    slots = device_index("ctx") ^ jnp.array(order, jnp.int32)
    return pl.pallas_call(
        body,
        out_shape=jax.ShapeDtypeStruct((seq, 2 * wide), jnp.bfloat16),
        in_specs=[pl.BlockSpec(memory_space=pltpu.SMEM)] + [vmem] * 11,
        out_specs=vmem,
        scratch_shapes=[pltpu.VMEM((seq, wide), jnp.float32)],
        compiler_params=pltpu.CompilerParams(vmem_limit_bytes=56 * 1024 * 1024),
        cost_estimate=cost(13),
        name="attention_back",
    )(
        slots, query, kv, heads, head_grads, totals, *tables, position[None, :],
        position[:, None],
    )


def local(
    hidden_in,
    out_cotangent,
    routes,
    route_probs,
    norm_gains,
    qkv_weight,
    out_weight,
    expert_up,
    expert_down,
    norm_gains_first,
    qkv_weight_first,
    out_weight_first,
    expert_up_first,
    expert_down_first,
    norm_gains_second,
    qkv_weight_second,
    out_weight_second,
    expert_up_second,
    expert_down_second,
):
    f32 = jnp.float32
    bf16 = jnp.bfloat16
    both = ("ctx", "fsdp")
    n_ctx = lax.axis_size("ctx")
    n_fsdp = lax.axis_size("fsdp")
    n_all = n_ctx * n_fsdp
    ctx_index = lax.axis_index("ctx")
    n_exp = expert_up.shape[0]
    shard = qkv_weight.shape[0]
    seq = DEVICE_TOKENS * n_ctx
    q_dev = QUERY_HEADS // n_ctx
    share = max(1, n_ctx // KEY_VALUE_HEADS)
    q_cols = q_dev * HEAD_SIZE
    kv_cols = HEAD_SIZE
    kv_from = 2 * HEAD_SIZE
    cols = 2 * kv_from

    tokens = hidden_in[0]
    cotangent = out_cotangent[0]

    expert_shards = [
        jnp.concatenate([expert_up[e].astype(bf16), expert_down[e].astype(bf16).T], 1)
        for e in range(n_exp)
    ]
    expert_shards[0], tokens = lax.optimization_barrier((expert_shards[0], tokens))
    expert_works = [lax.all_gather(part, "fsdp", axis=0, tiled=True) for part in expert_shards]
    inv_first = lax.rsqrt(jnp.mean(tokens * tokens, -1, keepdims=True) + NORM_EPS)
    unit_rows = (tokens * inv_first).astype(bf16)
    unit_all = gather_rows(unit_rows)

    gain_shard = norm_gains.astype(bf16).astype(f32)
    qkv_shard = qkv_weight.astype(bf16).astype(f32)
    scaled = (qkv_shard * gain_shard[0][:, None]).astype(bf16)
    q_part = scaled[:, :QUERY_FEATURES].reshape(shard, n_ctx, q_cols)
    k_part = scaled[:, QUERY_FEATURES : QUERY_FEATURES + KEY_FEATURES]
    v_part = scaled[:, QUERY_FEATURES + KEY_FEATURES :]
    k_part = jnp.repeat(k_part.reshape(shard, n_ctx // share, kv_cols), share, 1)
    v_part = jnp.repeat(v_part.reshape(shard, n_ctx // share, kv_cols), share, 1)
    q_part = jnp.pad(q_part, ((0, 0), (0, 0), (0, kv_from - q_cols)))
    head_cols = jnp.concatenate([q_part, k_part, v_part], -1).transpose(1, 0, 2)
    head_group = lax.all_to_all(head_cols, "ctx", split_axis=0, concat_axis=0, tiled=True)
    head_group = head_group.reshape(n_ctx * shard, cols)
    qkv_heads = assemble_heads(
        [head_group] + [exchange(head_group, "fsdp", mask) for mask in range(1, n_fsdp)], shard
    )

    gain_row = jnp.pad(norm_gains[1:2].astype(bf16), ((0, 7), (0, MODEL_WIDTH - shard)))
    out_shard = jnp.concatenate([out_weight.astype(bf16), gain_row], 0)
    out_group = [out_shard] + [exchange(out_shard, "fsdp", mask) for mask in range(1, n_fsdp)]

    experts = jnp.arange(n_exp * n_ctx, dtype=jnp.int32)
    chosen = routes[0][:, None, :] == experts[None, :, None]
    weight_rows = jnp.sum(jnp.where(chosen, route_probs[0][:, None, :], 0.0), 2).T
    weight_high = lax.reduce_precision(weight_rows, 8, 7)
    weight_low = weight_rows - weight_high
    weight_flat = jnp.stack([weight_high, weight_low]).reshape(-1, MODEL_WIDTH).astype(bf16)
    out_group, _ = lax.optimization_barrier((out_group, qkv_heads))
    gain_flat = jnp.concatenate([part[shard : shard + 1, :shard] for part in out_group], 1)
    gain_flat = jnp.pad(gain_flat, ((0, 0), (0, MODEL_WIDTH - n_fsdp * shard)))
    n_misc = weight_flat.shape[0]
    misc_rows = -(-(n_misc + 1) // 16) * 16
    payload = jnp.concatenate(
        [
            (RES_SCALE * cotangent).astype(bf16),
            *[part[:shard] for part in out_group],
            weight_flat,
            gain_flat,
            jnp.zeros((misc_rows - n_misc - 1, MODEL_WIDTH), bf16),
        ],
        0,
    )

    def out_place(mask_fsdp):
        def place(k, mask, ctx, fsdp):
            return ((ctx ^ mask) * n_fsdp + (fsdp ^ mask_fsdp)) * shard

        return place

    payload_pieces = row_pieces(payload)

    moves = [(0, DEVICE_TOKENS, 0, lambda k, mask, ctx, fsdp: k * DEVICE_TOKENS)]
    for mask_fsdp in range(n_fsdp):
        moves.append((DEVICE_TOKENS + mask_fsdp * shard, shard, 1, out_place(mask_fsdp)))
    moves.append(
        (DEVICE_TOKENS + q_cols, misc_rows, 2, lambda k, mask, ctx, fsdp: k * misc_rows)
    )
    device_ids = ctx_index ^ jnp.array(relative_order(n_ctx), jnp.int32)
    row_ids = device_ids[:, None] * DEVICE_TOKENS + jnp.arange(DEVICE_TOKENS, dtype=jnp.int32)
    position = positions(row_ids.reshape(-1), DEVICE_TOKENS, n_ctx)
    tables = rope_tables(position)

    queries, keys_values, attended, log_totals = attention(
        unit_all, qkv_heads, tables, position, q_dev, n_ctx
    )
    attended_natural = attended[:, :q_cols]
    attended_natural, payload_pieces = lax.optimization_barrier(
        (attended_natural, payload_pieces)
    )
    attn_rows = lax.all_to_all(attended_natural, "ctx", 0, 0, tiled=True)
    cotangent_all, out_all, misc_all = assemble(
        payload_pieces, [seq, MODEL_WIDTH, n_ctx * misc_rows], moves
    )
    misc_all = misc_all.reshape(n_ctx, misc_rows, MODEL_WIDTH)
    weight_all = (
        misc_all[:, :n_misc]
        .astype(f32)
        .reshape(n_ctx, 2, n_exp * n_ctx, DEVICE_TOKENS)
    )
    weight_all = lax.dynamic_slice_in_dim(
        weight_all[:, 0] + weight_all[:, 1], ctx_index * n_exp, n_exp, 1
    )
    weight_own = weight_all.transpose(0, 2, 1).reshape(seq, n_exp)
    gain_pieces = misc_all[:, n_misc, : n_fsdp * shard].astype(f32)
    group_ids = lax.axis_index("fsdp") ^ jnp.arange(n_fsdp, dtype=jnp.int32)
    piece_ids = (device_ids[:, None] * n_fsdp + group_ids[None, :]).reshape(n_all)
    is_piece = piece_ids[None, :] == jnp.arange(n_all, dtype=jnp.int32)[:, None]
    gain_ffn = jnp.sum(
        jnp.where(is_piece[:, :, None], gain_pieces.reshape(1, n_all, shard), 0.0), 1
    ).reshape(1, MODEL_WIDTH)

    residual, normed_ffn = project_out(attn_rows, out_all, tokens, gain_ffn)

    normed_all = gather_rows(normed_ffn)
    hidden = []
    expert_rows = []
    sums = [None]
    half = seq // 2
    for e in range(n_exp):
        weighted_hidden, pair_grad, *sums = expert_front(
            normed_all, cotangent_all, expert_works[e], weight_own[:, e : e + 1], sums[0]
        )
        if e == n_exp - 1:
            own_grad, grad_parts = pair_parts(*sums)
            grad_parts, weighted_hidden, pair_grad = lax.optimization_barrier(
                (grad_parts, weighted_hidden, pair_grad)
            )
            other_grads = send_parts(grad_parts)
        hidden.append(weighted_hidden)
        expert_term = expert_grads(normed_all, pair_grad, cotangent_all, weighted_hidden)
        if e < n_exp - 1:
            expert_works[e + 1], expert_term = lax.optimization_barrier(
                (expert_works[e + 1], expert_term)
            )
        expert_part = lax.psum_scatter(expert_term, "fsdp", scatter_dimension=0, tiled=True)
        expert_rows.append(with_layout_constraint(expert_part, Layout(major_to_minor=(0, 1))))
    value_sums = expert_value(hidden, expert_works)
    own_grad, value_sums = lax.optimization_barrier((own_grad, value_sums))

    residual_grad, attn_grad, gain_ffn_part, head_grads = residual_back(
        own_grad, other_grads, residual, cotangent, gain_ffn, out_all
    )
    gain_ffn_part = gain_ffn_part[0]
    hidden_out = residual + RES_SCALE * scatter_sum(*value_sums)
    attended_grad = lax.all_to_all(head_grads, "ctx", 0, 0, tiled=True)
    attended_grad = jnp.pad(attended_grad, ((0, 0), (0, kv_from - q_cols)))
    qkv_rows = attention_back(
        queries, keys_values, attended, attended_grad, log_totals, tables, position, q_dev, n_ctx
    )
    grad_all = gather_rows(attn_grad, True)
    out_term = lax.dot_general(
        attended_natural, grad_all, (((0,), (0,)), ((), ())), preferred_element_type=f32
    ).astype(bf16)
    out_term, qkv_rows = lax.optimization_barrier((out_term, qkv_rows))

    def in_grad_rows(rows):
        return lax.dot_general(
            rows, qkv_heads, (((1,), (1,)), ((), ())), preferred_element_type=f32
        )

    odd_in_grad = in_grad_rows(qkv_rows[half:]).astype(bf16)
    scaled_in_grad, in_parts = pair_parts(in_grad_rows(qkv_rows[:half]), odd_in_grad)
    in_parts, qkv_rows = lax.optimization_barrier((in_parts, qkv_rows))
    in_received = send_parts(in_parts)

    def update_expert(e, updates):
        return expert_update(
            e,
            expert_rows[e],
            (expert_up, expert_up_first, expert_up_second),
            (expert_down, expert_down_first, expert_down_second),
            updates,
        )

    updates = None
    for e in range(n_exp - 1):
        updates = update_expert(e, updates)
    scaled_in_grad = scaled_in_grad + in_received[0].astype(f32)
    updates, scaled_in_grad = lax.optimization_barrier((updates, scaled_in_grad))
    for part in in_received[1:]:
        scaled_in_grad = scaled_in_grad + part.astype(f32)
    input_grad = (
        residual_grad
        + inv_first * scaled_in_grad
        - tokens * inv_first**3 * jnp.mean(scaled_in_grad * tokens, -1, keepdims=True)
    )

    fsdp_index = lax.axis_index("fsdp")

    def out_block(mask):
        return lax.dynamic_slice_in_dim(out_term, (fsdp_index ^ mask) * shard, shard, 0)

    out_grad = out_block(0).astype(f32)
    for mask in range(1, n_fsdp):
        out_grad = out_grad + exchange(out_block(mask), "fsdp", mask).astype(f32)
    qkv_term = lax.dot_general(
        unit_all, qkv_rows, (((0,), (0,)), ((), ())), preferred_element_type=f32
    ).astype(bf16)
    gain_high = lax.reduce_precision(gain_ffn_part, 8, 7)
    gain_parts = jnp.stack([gain_high, gain_ffn_part - gain_high]).reshape(2, n_all, shard)
    gain_parts = jnp.pad(
        gain_parts.transpose(1, 0, 2).astype(bf16), ((0, 0), (0, 6), (0, cols - shard))
    )
    qkv_pieces = lax.all_to_all(
        jnp.concatenate([qkv_term.reshape(n_all, shard, cols), gain_parts], 1),
        both,
        0,
        0,
        tiled=True,
    ).reshape(n_ctx, n_fsdp, shard + 8, cols)
    gain_ffn_grad = jnp.sum(qkv_pieces[:, :, shard : shard + 2, :shard].astype(f32), (0, 1, 2))
    qkv_pieces = qkv_pieces[:, :, :shard]
    qkv_sum = jnp.sum(qkv_pieces.astype(f32), 1)
    kv_sum = jnp.sum(
        qkv_sum[..., kv_from:].reshape(n_ctx // share, share, shard, 2, kv_cols), 1
    ).transpose(1, 2, 0, 3)
    unit_grad = jnp.concatenate(
        [
            qkv_sum[..., :q_cols].transpose(1, 0, 2).reshape(shard, QUERY_FEATURES),
            kv_sum.reshape(shard, 2 * KEY_FEATURES),
        ],
        1,
    )
    qkv_grad = gain_shard[0][:, None] * unit_grad
    gain_attn_grad = jnp.sum(qkv_shard * unit_grad, 1)
    gains_grad = jnp.stack([gain_attn_grad, gain_ffn_grad])

    norm_new = adamw_update(norm_gains, gains_grad, norm_gains_first, norm_gains_second, 0.0)
    qkv_new = adamw_update(qkv_weight, qkv_grad, qkv_weight_first, qkv_weight_second, WEIGHT_DECAY)
    out_new = adamw_update(out_weight, out_grad, out_weight_first, out_weight_second, WEIGHT_DECAY)
    updates = update_expert(n_exp - 1, updates)
    up_grad_shard, *up_new = updates[:4]
    down_grad_shard, *down_new = updates[4:]
    return (
        hidden_out[None],
        input_grad[None],
        gains_grad,
        qkv_grad,
        out_grad,
        up_grad_shard,
        down_grad_shard,
        norm_new[0],
        qkv_new[0],
        out_new[0],
        up_new[0],
        down_new[0],
        norm_new[1],
        qkv_new[1],
        out_new[1],
        up_new[1],
        down_new[1],
        norm_new[2],
        qkv_new[2],
        out_new[2],
        up_new[2],
        down_new[2],
    )


def solution(mesh):
    in_specs = (
        P("fsdp", "ctx", None),
        P("fsdp", "ctx", None),
        P("fsdp", "ctx", None),
        P("fsdp", "ctx", None),
        P(None, ("ctx", "fsdp")),
        P(("ctx", "fsdp"), None),
        P(("ctx", "fsdp"), None),
        P("ctx", "fsdp", None),
        P("ctx", None, "fsdp"),
        P(None, ("ctx", "fsdp")),
        P(("ctx", "fsdp"), None),
        P(("ctx", "fsdp"), None),
        P("ctx", "fsdp", None),
        P("ctx", None, "fsdp"),
        P(None, ("ctx", "fsdp")),
        P(("ctx", "fsdp"), None),
        P(("ctx", "fsdp"), None),
        P("ctx", "fsdp", None),
        P("ctx", None, "fsdp"),
    )
    out_specs = (
        P("fsdp", "ctx", None),
        P("fsdp", "ctx", None),
        P(None, ("ctx", "fsdp")),
        P(("ctx", "fsdp"), None),
        P(("ctx", "fsdp"), None),
        P("ctx", "fsdp", None),
        P("ctx", None, "fsdp"),
        P(None, ("ctx", "fsdp")),
        P(("ctx", "fsdp"), None),
        P(("ctx", "fsdp"), None),
        P("ctx", "fsdp", None),
        P("ctx", None, "fsdp"),
        P(None, ("ctx", "fsdp")),
        P(("ctx", "fsdp"), None),
        P(("ctx", "fsdp"), None),
        P("ctx", "fsdp", None),
        P("ctx", None, "fsdp"),
        P(None, ("ctx", "fsdp")),
        P(("ctx", "fsdp"), None),
        P(("ctx", "fsdp"), None),
        P("ctx", "fsdp", None),
        P("ctx", None, "fsdp"),
    )

    return jax.shard_map(local, mesh=mesh, in_specs=in_specs, out_specs=out_specs, check_vma=False)
```
